512 devices in a mesh: dp: 64 (over z, y_hi, core), chan: 8 (over x, y_lo).
Axes of the slice: x: 4, y: 4 (y_hi: 2, y_lo: 2; y = y_hi * 2 + y_lo), z: 16, core: 2. Of those that a mesh axis runs over, the one named last changes fastest.
Arguments:
- h_in: bfloat16 [64, 1280, 1024], P('dp', 'chan'), may hold values from -40 to 40
- skip: bfloat16 [64, 1280, 1024], P('dp', 'chan'), may hold values from -6 to 6
- emb: bfloat16 [64, 1280], P('dp'), may hold values from -6 to 6
- w_emb: bfloat16 [1280, 1280], P('dp', 'chan'), may hold values from -0.15625 to 0.15625
- b_emb: float32 [1280], P('chan'), may hold values from -3 to 3
- gn_gain: float32 [1280], P('chan'), may hold values from 0.1 to 1.9
- gn_bias: float32 [1280], P('chan'), may hold values from -3 to 3
- w_conv: bfloat16 [9, 1280, 1280], P(None, 'dp', 'chan'), may hold values from -0.0546875 to 0.0546875
- b_conv: float32 [1280], P('chan'), may hold values from -3 to 3
Outputs:
- block_out: bfloat16 [64, 1280, 1024], P('dp', 'chan')
The draws below stay inside these ranges and needn't reach their ends.
All inputs are finite; a program needn't handle non-finite values.
Results may differ from the reference program's by a relative error of at most 0.0036.
Values may be sent and summed in bfloat16 or wider, within the bound.
A program may use at most 128 MiB of HBM per device.

```python
import jax
import jax.numpy as jnp
from jax import lax

C = 1280
GROUPS = 32
C_EMB = 1280
HEIGHT = 32
WIDTH = 32
BATCH = 64
HW = 1024


def draw_h_in(key, part):
    keys = jax.random.split(jax.random.fold_in(key, 17), 3)
    span = jnp.log(10.0)
    channel_scale = jnp.exp(jax.random.uniform(keys[1], (1, C, 1), jnp.float32, 0.0, span))
    place_scale = jnp.exp(jax.random.uniform(keys[2], (1, 1, HEIGHT * WIDTH), jnp.float32, 0.0, span))
    scale = channel_scale * place_scale / 10.0
    base = jax.random.truncated_normal(keys[0], -4.0, 4.0, (BATCH, C, HEIGHT * WIDTH), jnp.float32)
    return (base * scale).astype(jnp.bfloat16)


def levels(rng, dims, pieces, smallest, high):
    level = 1.0
    for dim, blocks in pieces:
        steps = jax.random.uniform(jax.random.fold_in(jax.random.fold_in(rng, 6), dim), (blocks,), jnp.float32, smallest / len(pieces), high / len(pieces))
        level = level * jnp.repeat(jnp.exp(steps), dims[dim] // blocks).reshape((-1,) + (1,) * (len(dims) - 1 - dim))
    return level


def scatter_about(rng, dims, width, bound, cuts=(), dtype=jnp.bfloat16):
    values = width * jax.random.normal(rng, dims, jnp.float32)
    if cuts:
        values = values * levels(rng, dims, cuts, -0.22, 0.18)
    return jnp.clip(values, -bound, bound).astype(dtype)


def setup_inputs(seed: int = 0) -> dict:
    arg_keys = jax.random.split(jax.random.key(seed), 10)
    return {
        "h_in": draw_h_in(jax.random.fold_in(arg_keys[9], 71), 0),
        "skip": scatter_about(arg_keys[1], (BATCH, C, HW), 1.0, 6.0, ((0, 64), (1, 8))),
        "emb": scatter_about(arg_keys[2], (BATCH, C_EMB), 1.0, 6.0, ((0, 64),)),
        "w_emb": scatter_about(arg_keys[3], (C_EMB, C), C_EMB ** -0.5, 0.15625, ((0, 64), (1, 8))),
        "b_emb": scatter_about(arg_keys[4], (C,), 0.5, 3.0, ((0, 8),), jnp.float32),
        "gn_gain": jnp.clip(1.0 + 0.18 * jax.random.normal(arg_keys[5], (C,), jnp.float32), 0.1, 1.9),
        "gn_bias": scatter_about(arg_keys[6], (C,), 0.5, 3.0, ((0, 8),), jnp.float32),
        "w_conv": scatter_about(arg_keys[7], (9, C, C), (9 * C) ** -0.5, 0.0546875, ((1, 64), (2, 8))),
        "b_conv": scatter_about(arg_keys[8], (C,), 0.5, 3.0, ((0, 8),), jnp.float32),
    }


def convolve(image, w_conv):
    grid = image.astype(jnp.float32).reshape(C, HEIGHT, WIDTH)
    padded = jnp.pad(grid, ((0, 0), (1, 1), (1, 1)))
    total = jnp.zeros((C, HEIGHT * WIDTH), jnp.float32)
    for row_off in range(3):
        for col_off in range(3):
            window = padded[:, row_off:row_off + HEIGHT, col_off:col_off + WIDTH].reshape(C, HEIGHT * WIDTH)
            weights = w_conv[3 * row_off + col_off].astype(jnp.float32)
            total = total + jnp.einsum('io,ip->op', weights, window, precision=lax.Precision.HIGHEST)
    return total

def reference(h_in, skip, emb, w_emb, b_emb, gn_gain, gn_bias, w_conv, b_conv):
    act = jax.nn.silu(emb.astype(jnp.float32)).astype(jnp.bfloat16)
    shift = jnp.dot(act, w_emb, preferred_element_type=jnp.float32) + b_emb
    hidden = h_in.astype(jnp.float32) + shift[:, :, None]
    grouped = hidden.reshape(BATCH, GROUPS, C // GROUPS, HEIGHT * WIDTH)
    mean = lax.optimization_barrier(jnp.mean(grouped, axis=(2, 3), keepdims=True))
    var = lax.optimization_barrier(jnp.mean((grouped - mean) ** 2, axis=(2, 3), keepdims=True))
    scaled = ((grouped - mean) * lax.rsqrt(var + 1e-05)).reshape(BATCH, C, HEIGHT * WIDTH)
    normed = jax.nn.silu(scaled * gn_gain[:, None] + gn_bias[:, None]).astype(jnp.bfloat16)
    conv = lax.map(lambda image: convolve(image, w_conv), normed)
    conv = conv + b_conv[None, :, None]
    return (skip.astype(jnp.float32) + conv).astype(jnp.bfloat16)
```

```python
import jax
import jax.numpy as jnp
from jax import lax
from jax.experimental import pallas as pl
from jax.experimental.pallas import tpu as pltpu
from jax.sharding import PartitionSpec as P

MESH = pl.DeviceIdType.MESH
F32 = jnp.float32
BF16 = jnp.bfloat16

NZ = 16
TILES = 13
SLOT = 80
PIECE = 272
ROWS = 1280
HALF = 640
PAD = 40
CHUNKS = ((0, 2), (2, 5), (7, 6))


def lane_iota(rows):
    return lax.broadcasted_iota(jnp.int32, (rows, 128), 1)


def kernel(
    h_ref, skip_ref, emb_ref, wemb_ref, prm_ref, w_ref, out_ref,
    hown, pbuf, pf, mf, wbuf, wk, abuf, nt, sbuf, abv, z_ref,
    p_send, p_recv, r_send, r_recv, c_send, c_recv, a_send, a_recv, b_send, b_recv,
):
    dp = lax.axis_index("dp")
    chan = lax.axis_index("chan")
    z = dp // 4
    yhi = (dp // 2) % 2
    core = dp % 2
    x = chan // 2
    ylo = chan % 2
    sgn = 1 - 2 * core

    def dp_at(zz, yy, cc):
        return zz * 4 + yy * 2 + cc

    z_next = dp_at((z + sgn + NZ) % NZ, yhi, core)
    z_prev = dp_at((z - sgn + NZ) % NZ, yhi, core)
    dp_core = dp_at(z, yhi, 1 - core)
    dp_yhi = dp_at(z, 1 - yhi, core)
    xr = (x + 1) % 4
    xl = (x + 3) % 4
    xo = (x + 2) % 4
    yb = 1 - ylo

    def ch(xx, yy):
        return xx * 2 + yy

    barrier = pltpu.get_barrier_semaphore()
    for d in (z_next, z_prev, dp_core, dp_yhi):
        pl.semaphore_signal(barrier, inc=1, device_id=(d, chan), device_id_type=MESH)
    for k in range(1, 8):
        pl.semaphore_signal(barrier, inc=1, device_id=(dp, (chan + k) % 8), device_id_type=MESH)

    def rcopy(src, dst, ssem, rsem, dev):
        return pltpu.make_async_remote_copy(
            src_ref=src, dst_ref=dst, send_sem=ssem, recv_sem=rsem,
            device_id=dev, device_id_type=MESH,
        )

    q = 2 * yhi + core
    pf[0, 256:272, :] = jnp.zeros((16, 128), F32)
    emb_w = wemb_ref[...].astype(F32)
    pf[0, 0:20, :] = emb_w[:, 0:128]
    for dy in range(3):
        taps = [w_ref[3 * dy + dx].astype(F32) for dx in range(3)]
        last = emb_w[:, 128:160] if dy == 0 else jnp.zeros((20, 32), F32)
        pf[0, 20 * (1 + dy):20 * (2 + dy), :] = jnp.concatenate(
            [t[:, 128:160] for t in taps] + [last], axis=1)
        for dx in range(3):
            t = 4 + 3 * dy + dx
            pf[0, 20 * t:20 * t + 20, :] = taps[dx][:, 0:128]
    pbuf[q] = pf[0].astype(BF16)

    for k in range(8):
        blk = h_ref[0:128, 128 * k:128 * k + 128].astype(F32)
        hown[128 * k:128 * k + 128, :] = blk.T.astype(BF16)
    for k in range(2):
        blk = jnp.concatenate(
            [h_ref[128:160, 256 * m + 128 * k:256 * m + 128 * k + 128] for m in range(4)],
            axis=0).astype(F32)
        hown[1024 + 128 * k:1024 + 128 * k + 128, :] = blk.T.astype(BF16)

    pl.semaphore_wait(barrier, 11)

    q_y = 2 * (1 - yhi) + core
    q_c = 2 * yhi + (1 - core)
    q_yc = 2 * (1 - yhi) + (1 - core)

    def piece(src_slot, dev, i):
        return rcopy(pbuf.at[src_slot], pbuf.at[src_slot], p_send.at[i], p_recv.at[i], (dev, chan))

    to_y = piece(q, dp_yhi, 0)
    to_y.start()
    to_c = piece(q, dp_core, 1)
    to_c.start()

    def act(src, slot, half, dev_chan, i):
        rows = pl.ds(HALF * half, HALF)
        return rcopy(src.at[rows, :], abuf.at[slot, rows, :], a_send.at[i], a_recv.at[i], (dp, dev_chan))

    sent = []
    me = ch(x, ylo)

    def go(copy):
        copy.start()
        sent.append(copy)

    go(act(hown, me, 0, ch(xr, ylo), 0))
    go(act(hown, me, 1, ch(xl, ylo), 3))
    go(act(hown, me, 0, ch(x, yb), 4))
    go(act(hown, me, 1, ch(xr, ylo), 1))
    go(act(hown, me, 0, ch(xl, ylo), 2))
    go(act(hown, me, 1, ch(x, yb), 5))

    def got(slot, half, i):
        rows = pl.ds(HALF * half, HALF)
        return rcopy(abuf.at[slot, rows, :], abuf.at[slot, rows, :], a_send.at[i], a_recv.at[i], (dp, ch(xr, ylo)))

    to_y.wait_recv()
    fwd = piece(q_y, dp_core, 2)
    fwd.start()
    to_c.wait_recv()
    fwd.wait_recv()
    for i in range(4):
        pf[i] = pbuf[i].astype(F32)
    for t in range(TILES):
        for i in range(4):
            mf[t, 20 * i:20 * i + 20, :] = pf[i, 20 * t:20 * t + 20, :]
    wbuf[z] = mf[...].astype(BF16)

    def ring(c, s):
        t0, n = CHUNKS[c]
        slot = (z - sgn * (s - 1) + 2 * NZ) % NZ
        ref = wbuf.at[slot, pl.ds(t0, n)]
        return rcopy(ref, ref, r_send.at[c, s - 1], r_recv.at[c, s - 1], (z_next, chan))

    def across(c, s):
        t0, n = CHUNKS[c]
        slot = (z - sgn * s + 2 * NZ) % NZ
        ref = wbuf.at[slot, pl.ds(t0, n)]
        return rcopy(ref, ref, c_send.at[c, s - 1], c_recv.at[c, s - 1], (dp_core, chan))

    def across_in(c, s):
        t0, n = CHUNKS[c]
        slot = (z + sgn * s + 2 * NZ) % NZ
        ref = wbuf.at[slot, pl.ds(t0, n)]
        return rcopy(ref, ref, c_send.at[c, s - 1], c_recv.at[c, s - 1], (dp_core, chan))

    def ring_in(c, s):
        t0, n = CHUNKS[c]
        slot = (z - sgn * s + 2 * NZ) % NZ
        ref = wbuf.at[slot, pl.ds(t0, n)]
        return rcopy(ref, ref, r_send.at[c, s - 1], r_recv.at[c, s - 1], (z_next, chan))

    def last_side(c):
        return core == (1 if c == 2 else 0)

    for c in range(3):
        ring(c, 1).start()

    def ring_step(c, s):
        def body():
            ring_in(c, s).wait_recv()
            across(c, s).start()
        if s < 8:
            ring_in(c, s).wait_recv()
            if s + 1 < 8:
                ring(c, s + 1).start()
            else:
                @pl.when(last_side(c))
                def _():
                    ring(c, 8).start()
            across(c, s).start()
        else:
            pl.when(last_side(c))(body)

    def stats():
        def total(lo, n, centre):
            def step(k, acc):
                v = hown[pl.ds(pl.multiple_of(lo + 128 * k, 128), 128), :].astype(F32)
                if centre is not None:
                    v = v - centre
                    v = v * v
                return acc + jnp.sum(v.reshape(16, 8, 128), axis=0)
            acc = lax.fori_loop(0, n, step, jnp.zeros((8, 128), F32))
            return jnp.sum(acc, axis=0, keepdims=True)

        def fold(v):
            v = v + pltpu.roll(v, 64, 1)
            return v + pltpu.roll(v, 32, 1)

        def fold1(v):
            return fold(jnp.broadcast_to(v, (8, 128)))[0:1, :]

        m_main = total(0, 8, None) * (1.0 / 1024.0)
        m_res = fold1(total(1024, 2, None)) * (1.0 / 1024.0)
        v_main = total(0, 8, m_main) * (1.0 / 1024.0)
        v_res = fold1(total(1024, 2, m_res)) * (1.0 / 1024.0)
        return m_main, m_res, v_main, v_res, fold1

    m_main, m_res, v_main, v_res, fold1 = stats()

    def affine():
        e = emb_ref[...].astype(F32)
        a = (e / (1.0 + jnp.exp(-e))).astype(BF16)
        lhs = jnp.broadcast_to(a, (16, 1280))
        rhs = jnp.concatenate(
            [wbuf[:, 0].reshape(NZ * SLOT, 128), wbuf[:, 1].reshape(NZ * SLOT, 128)], axis=1)
        prod = jnp.dot(lhs, rhs, preferred_element_type=F32)
        lane = lane_iota(1)
        prm = prm_ref[...]
        prm_res = jnp.concatenate([prm[:, 128:160]] * 4, axis=1)
        s_main = prod[0:1, 0:128] + prm[0:1, 0:128]
        s_res = fold1(jnp.where(lane >= 96, prod[0:1, 128:256], 0.0)) + prm_res[0:1]
        u_main = m_main + s_main
        u_res = m_res + s_res

        def group(main, res):
            out_main = jnp.zeros((1, 128), F32)
            for g in range(3):
                inside = (lane >= 40 * g) & (lane < 40 * g + 40)
                t = jnp.sum(jnp.where(inside, main, 0.0), axis=1, keepdims=True) * (1.0 / 40.0)
                out_main = jnp.where(inside, t, out_main)
            t = jnp.sum(jnp.where(lane >= 120, main, 0.0) + jnp.where(lane < 32, res, 0.0),
                        axis=1, keepdims=True) * (1.0 / 40.0)
            return jnp.where(lane >= 120, t, out_main), jnp.broadcast_to(t, (1, 128))

        mean_main, mean_res = group(u_main, u_res)
        d_main = u_main - mean_main
        d_res = u_res - mean_res
        var_main, var_res = group(v_main + d_main * d_main, v_res + d_res * d_res)
        a_main = prm[1:2, 0:128] * lax.rsqrt(var_main + 1e-5)
        a_res = prm_res[1:2] * lax.rsqrt(var_res + 1e-5)
        b_main = prm[2:3, 0:128] + (s_main - mean_main) * a_main
        b_res = prm_res[2:3] + (s_res - mean_res) * a_res
        abv[me] = jnp.concatenate(
            [a_main, b_main, a_res, b_res, jnp.zeros((4, 128), F32)], axis=0)

    def ab_copy(k):
        return rcopy(abv.at[me], abv.at[me], b_send.at[k - 1], b_recv.at[k - 1], (dp, (chan + k) % 8))

    def ab_in(k):
        slot = (chan - k + 8) % 8
        return rcopy(abv.at[slot], abv.at[slot], b_send.at[k - 1], b_recv.at[k - 1], (dp, (chan + k) % 8))

    def normalise(src, slot):
        ab = abv[slot]

        def silu(v, a, b):
            v = v.astype(F32) * a + b
            half = 0.5 * v
            return half + half * jnp.tanh(half)

        lanes = pl.ds(pl.multiple_of(slot * 128, 128), 128)

        def step(k, carry):
            rows = pl.ds(pl.multiple_of(128 * k, 128), 128)
            nt[rows, lanes] = silu(src[rows, :], ab[0:1], ab[1:2]).astype(BF16)
            return carry
        lax.fori_loop(0, 8, step, 0)

        def step_res(k, carry):
            rows = pl.ds(pl.multiple_of(1024 + 128 * k, 128), 128)
            sbuf[slot, pl.ds(pl.multiple_of(128 * k, 128), 128), :] = silu(src[rows, :], ab[2:3], ab[3:4])
            return carry
        lax.fori_loop(0, 2, step_res, 0)

    def place(slot, c):
        t0, n = CHUNKS[c]
        j = slot // 2
        odd = slot % 2
        lo = pl.multiple_of(128 * j + 80 * odd, 16)
        hi = pl.multiple_of((1 - odd) * (128 * j + 48) + odd * (1024 + 32 * j), 16)
        for t in range(max(t0, 1), t0 + n):
            cols = slice(128 * (t - 1), 128 * t)
            wk[pl.ds(lo, 48), cols] = wbuf[slot, t, 0:48, :]
            wk[pl.ds(hi, 32), cols] = wbuf[slot, t, 48:80, :]

    def place_all(s):
        for side in (-1, 1):
            slot = (z + side * sgn * s + 2 * NZ) % NZ
            for c in range(3):
                place(slot, c)

    def across_wait(c, s):
        if s < 8:
            across_in(c, s).wait_recv()
        else:
            pl.when(core == (0 if c == 2 else 1))(lambda: across_in(c, s).wait_recv())

    xlb, xrb, yb_, ob = ch(xl, ylo), ch(xr, ylo), ch(x, yb), ch(xo, ylo)
    lyb, ryb, oyb = ch(xl, yb), ch(xr, yb), ch(xo, yb)

    for c in range(3):
        place(z, c)

    for s in range(1, 9):
        for sa in (2 * s - 1, 2 * s):
            if sa <= 8:
                ring_step(0, sa)
                across_wait(0, sa)
        ring_step(1, s)
        ring_step(2, s)
        if s == 1:
            got(xlb, 0, 0).wait_recv()
            go(act(abuf.at[xlb], xlb, 0, ch(xr, ylo), 6))
            got(xrb, 1, 3).wait_recv()
            go(act(abuf.at[xrb], xrb, 1, ch(xl, ylo), 7))
            got(yb_, 0, 4).wait_recv()
            go(act(abuf.at[yb_], yb_, 0, ch(xr, ylo), 8))
            go(act(abuf.at[yb_], yb_, 0, ch(xl, ylo), 10))
        if s == 2:
            got(yb_, 1, 5).wait_recv()
            go(act(abuf.at[yb_], yb_, 1, ch(xr, ylo), 9))
            go(act(abuf.at[yb_], yb_, 1, ch(xl, ylo), 11))
        if s == 3:
            got(ob, 0, 6).wait_recv()
            go(act(abuf.at[ob], ob, 0, ch(x, yb), 12))
            got(ob, 1, 7).wait_recv()
            go(act(abuf.at[ob], ob, 1, ch(x, yb), 13))
        if s == 4:
            affine()
            for k in range(1, 8):
                ab_copy(k).start()
            normalise(hown, me)
        if s == 5:
            for k in range(1, 8):
                ab_in(k).wait_recv()
            got(xlb, 1, 1).wait_recv()
            normalise(abuf.at[xlb], xlb)
            got(xrb, 0, 2).wait_recv()
            normalise(abuf.at[xrb], xrb)
        if s == 6:
            normalise(abuf.at[yb_], yb_)
            normalise(abuf.at[ob], ob)
        if s == 7:
            got(lyb, 0, 8).wait_recv()
            got(lyb, 1, 9).wait_recv()
            normalise(abuf.at[lyb], lyb)
            got(ryb, 0, 10).wait_recv()
            got(ryb, 1, 11).wait_recv()
            normalise(abuf.at[ryb], ryb)
        if s > 1:
            across_wait(1, s - 1)
            across_wait(2, s - 1)
            place_all(s - 1)
    got(oyb, 0, 12).wait_recv()
    got(oyb, 1, 13).wait_recv()
    normalise(abuf.at[oyb], oyb)
    across_wait(1, 8)
    across_wait(2, 8)
    for c in range(3):
        place((z + 8) % NZ, c)

    lane = lane_iota(256)
    for k in range(4):
        for half in range(2):
            acc = jnp.zeros((256, 128), F32)
            for m in range(4):
                v = sbuf[4 * half + m]
                shift = (32 * (m - k)) % 128
                if shift:
                    v = pltpu.roll(v, shift, 1)
                acc = jnp.where((lane >= 32 * m) & (lane < 32 * m + 32), v, acc)
            nt[256 * k:256 * k + 256, 1024 + 128 * half:1152 + 128 * half] = acc.astype(BF16)

    z_ref[0:PAD, :] = jnp.zeros((PAD, 1536), F32)
    z_ref[PAD + 1024:PAD + 1024 + PAD, :] = jnp.zeros((PAD, 1536), F32)

    def mm(n, carry):
        cols = pl.ds(pl.multiple_of(256 * n, 256), 256)
        z_ref[PAD:PAD + 1024, cols] = jnp.dot(nt[...], wk[:, cols], preferred_element_type=F32)
        return carry
    lax.fori_loop(0, 6, mm, 0)

    bias_main = prm_ref[3:4, 0:128]
    bias_res = jnp.concatenate([prm_ref[3:4, 128:160]] + [jnp.zeros((1, 96), F32)], axis=1)
    row = lax.broadcasted_iota(jnp.int32, (128, 128), 0) % 32
    lane = lane_iota(128)
    for k in range(8):
        base = PAD + 128 * k

        def band(tile, off):
            return z_ref[base + off:base + off + 128, 128 * tile:128 * tile + 128]

        side = [jnp.zeros((128, 128), F32)] * 3
        for dx in range(3):
            for dy in range(3):
                side[dx] = side[dx] + band(3 + 3 * dy + dx, 32 * (dy - 1) + dx - 1)
        main = side[1] + jnp.where(row > 0, side[0], 0.0) + jnp.where(row < 31, side[2], 0.0)
        res = [sum(band(dy, 32 * (dy - 1) + off) for dy in range(3)) for off in (-1, 0, 1)]
        u = jnp.where(lane < 32, jnp.where(row > 0, res[0], 0.0),
                      jnp.where(lane < 64, res[1],
                                jnp.where((lane < 96) & (row < 31), res[2], 0.0)))
        u = u + pltpu.roll(u, 96, 1) + pltpu.roll(u, 64, 1)
        cols = slice(128 * k, 128 * k + 128)
        out_ref[0:128, cols] = (skip_ref[0:128, cols].astype(F32) + (main + bias_main).T).astype(BF16)
        tail = (u + bias_res).T
        out_ref[128:160, cols] = (skip_ref[128:160, cols].astype(F32) + tail[0:32, :]).astype(BF16)

    to_y.wait_send()
    to_c.wait_send()
    fwd.wait_send()
    for copy in sent:
        copy.wait_send()
    for k in range(1, 8):
        ab_copy(k).wait_send()
    for c in range(3):
        for s in range(1, 9):
            if s < 8:
                ring(c, s).wait_send()
                across(c, s).wait_send()
            else:
                @pl.when(last_side(c))
                def _():
                    ring(c, 8).wait_send()
                    across(c, 8).wait_send()


def body(h_in, skip, emb, w_emb, b_emb, gn_gain, gn_bias, w_conv, b_conv):
    prm = jnp.stack([b_emb, gn_gain, gn_bias, b_conv])
    vmem = pl.BlockSpec(memory_space=pltpu.VMEM)
    dma = pltpu.SemaphoreType.DMA
    out = pl.pallas_call(
        kernel,
        out_shape=jax.ShapeDtypeStruct((160, 1024), BF16),
        in_specs=[vmem] * 6,
        out_specs=vmem,
        scratch_shapes=[
            pltpu.VMEM((ROWS, 128), BF16),
            pltpu.VMEM((4, PIECE, 128), BF16),
            pltpu.VMEM((4, PIECE, 128), F32),
            pltpu.VMEM((TILES, SLOT, 128), F32),
            pltpu.VMEM((NZ, TILES, SLOT, 128), BF16),
            pltpu.VMEM((1280, 1536), BF16),
            pltpu.VMEM((8, ROWS, 128), BF16),
            pltpu.VMEM((1024, 1280), BF16),
            pltpu.VMEM((8, 256, 128), F32),
            pltpu.VMEM((8, 8, 128), F32),
            pltpu.VMEM((1024 + 2 * PAD, 1536), F32),
            dma((3,)), dma((3,)),
            dma((3, 8)), dma((3, 8)),
            dma((3, 8)), dma((3, 8)),
            dma((14,)), dma((14,)),
            dma((7,)), dma((7,)),
        ],
        compiler_params=pltpu.CompilerParams(
            collective_id=0, has_side_effects=True, vmem_limit_bytes=52 << 20),
        name="resblock",
    )(h_in[0], skip[0], emb, w_emb, prm, w_conv)
    return out[None]


def solution(mesh):
    return jax.shard_map(
        body,
        mesh=mesh,
        in_specs=(
            P("dp", "chan", None),
            P("dp", "chan", None),
            P("dp", None),
            P("dp", "chan"),
            P("chan"),
            P("chan"),
            P("chan"),
            P(None, "dp", "chan"),
            P("chan"),
        ),
        out_specs=P("dp", "chan", None),
        check_vma=False,
    )
```

```python
import jax
import jax.numpy as jnp
from jax import lax
from jax.experimental import pallas as pl
from jax.experimental.pallas import tpu as pltpu
from jax.sharding import PartitionSpec as P

MESH = pl.DeviceIdType.MESH
F32 = jnp.float32
BF16 = jnp.bfloat16

NZ = 16
TILES = 12
SLOT = 80
PIECE = 288
ROWS = 1280
HALF = 640
PAD = 40
NC = 6
CT = TILES // NC


def lane_iota(rows):
    return lax.broadcasted_iota(jnp.int32, (rows, 128), 1)


def kernel(
    h_hbm, skip_hbm, emb_ref, wemb_hbm, prm_ref, w_hbm, out_ref,
    h_ref, skip_ref, wemb_ref, w_ref,
    hown, pbuf, pf, mf, wbuf, wk, abuf, nt, sbuf, abv, z_ref,
    actv, e_act, e_w, e_part, e_sum,
    in_sem, p_send, p_recv, r_send, r_recv, c_send, c_recv, a_send, a_recv, b_send, b_recv,
    e_send, e_recv, f_send, f_recv,
):
    dp = lax.axis_index("dp")
    chan = lax.axis_index("chan")
    z = dp // 4
    yhi = (dp // 2) % 2
    core = dp % 2
    x = chan // 2
    ylo = chan % 2
    sgn = 1 - 2 * core

    loads = [
        pltpu.make_async_copy(w_hbm, w_ref, in_sem.at[0]),
        pltpu.make_async_copy(wemb_hbm, wemb_ref, in_sem.at[1]),
        pltpu.make_async_copy(h_hbm.at[0], h_ref, in_sem.at[2]),
        pltpu.make_async_copy(skip_hbm.at[0], skip_ref, in_sem.at[3]),
    ]
    for load in loads:
        load.start()

    def dp_at(zz, yy, cc):
        return zz * 4 + yy * 2 + cc

    z_next = dp_at((z + sgn + NZ) % NZ, yhi, core)
    z_skip = dp_at((z + 2 * sgn + NZ) % NZ, yhi, core)
    dp_core = dp_at(z, yhi, 1 - core)
    dp_yhi = dp_at(z, 1 - yhi, core)
    xr = (x + 1) % 4
    xl = (x + 3) % 4
    xo = (x + 2) % 4
    yb = 1 - ylo

    def ch(xx, yy):
        return xx * 2 + yy

    barrier = pltpu.get_barrier_semaphore()
    for d in [dp_core, dp_yhi] + [dp_at((z + k) % NZ, yhi, core) for k in range(1, NZ)]:
        pl.semaphore_signal(barrier, inc=1, device_id=(d, chan), device_id_type=MESH)
    for k in range(1, 8):
        pl.semaphore_signal(barrier, inc=1, device_id=(dp, (chan + k) % 8), device_id_type=MESH)

    def rcopy(src, dst, ssem, rsem, dev):
        return pltpu.make_async_remote_copy(
            src_ref=src, dst_ref=dst, send_sem=ssem, recv_sem=rsem,
            device_id=dev, device_id_type=MESH,
        )

    q = 2 * yhi + core
    pf[0, 272:288, :] = jnp.zeros((16, 128), F32)
    loads[0].wait()
    loads[1].wait()
    for dy in range(3):
        taps = [w_ref[3 * dy + dx].astype(F32) for dx in range(3)]
        pf[0, 20 * dy:20 * dy + 20, :] = jnp.concatenate(
            [t[:, 128:160] for t in taps] + [jnp.zeros((20, 32), F32)], axis=1)
        for dx in range(3):
            t = 3 + 3 * dy + dx
            pf[0, 20 * t:20 * t + 20, :] = taps[dx][:, 0:128]
    emb_w = wemb_ref[...].astype(F32)
    pf[0, 240:260, :] = emb_w[:, 0:128]
    pf[0, 260:280, :] = jnp.concatenate([emb_w[:, 128:160], jnp.zeros((20, 96), F32)], axis=1)
    pbuf[q] = pf[0].astype(BF16)

    e = emb_ref[...].astype(F32)
    actv[:, 0:1280] = (e / (1.0 + jnp.exp(-e))).astype(BF16).astype(F32)
    actv[:, 1280:1408] = jnp.zeros((1, 128), F32)

    def window(zz):
        return pl.ds(pl.multiple_of(128 * ((80 * zz) // 128), 128), 256)

    e_act[z] = actv[:, window(z)]
    e_w[...] = jnp.zeros((256, 256), BF16)

    pl.semaphore_wait(barrier, 24)

    q_y = 2 * (1 - yhi) + core
    q_c = 2 * yhi + (1 - core)
    q_yc = 2 * (1 - yhi) + (1 - core)

    def piece(src_slot, dev, i):
        return rcopy(pbuf.at[src_slot], pbuf.at[src_slot], p_send.at[i], p_recv.at[i], (dev, chan))

    to_y = piece(q, dp_yhi, 0)
    to_y.start()
    to_c = piece(q, dp_core, 1)
    to_c.start()

    def emb_copy(k):
        zz = (z + k) % NZ
        return rcopy(actv.at[:, window(zz)], e_act.at[z], e_send.at[k - 1], e_recv.at[k - 1], (dp_at(zz, yhi, core), chan))

    def emb_in(k):
        slot = (z - k + NZ) % NZ
        return rcopy(e_act.at[slot], e_act.at[slot], e_send.at[k - 1], e_recv.at[k - 1], (dp_core, chan))

    def part_copy(k):
        zz = (z + k) % NZ
        return rcopy(e_part.at[zz], e_sum.at[z], f_send.at[k - 1], f_recv.at[k - 1], (dp_at(zz, yhi, core), chan))

    def part_in(k):
        slot = (z - k + NZ) % NZ
        return rcopy(e_sum.at[slot], e_sum.at[slot], f_send.at[k - 1], f_recv.at[k - 1], (dp_core, chan))

    for k in range(1, NZ):
        emb_copy(k).start()

    loads[2].wait()
    for k in range(8):
        blk = h_ref[0:128, 128 * k:128 * k + 128].astype(F32)
        hown[128 * k:128 * k + 128, :] = blk.T.astype(BF16)
    for k in range(2):
        blk = jnp.concatenate(
            [h_ref[128:160, 256 * m + 128 * k:256 * m + 128 * k + 128] for m in range(4)],
            axis=0).astype(F32)
        hown[1024 + 128 * k:1024 + 128 * k + 128, :] = blk.T.astype(BF16)


    def act(src, slot, half, dev_chan, i):
        rows = pl.ds(HALF * half, HALF)
        return rcopy(src.at[rows, :], abuf.at[slot, rows, :], a_send.at[i], a_recv.at[i], (dp, dev_chan))

    sent = []
    me = ch(x, ylo)

    def go(copy):
        copy.start()
        sent.append(copy)

    go(act(hown, me, 0, ch(xr, ylo), 0))
    go(act(hown, me, 1, ch(xl, ylo), 3))
    go(act(hown, me, 0, ch(x, yb), 4))
    go(act(hown, me, 1, ch(xr, ylo), 1))
    go(act(hown, me, 0, ch(xl, ylo), 2))
    go(act(hown, me, 1, ch(x, yb), 5))

    def got(slot, half, i):
        rows = pl.ds(HALF * half, HALF)
        return rcopy(abuf.at[slot, rows, :], abuf.at[slot, rows, :], a_send.at[i], a_recv.at[i], (dp, ch(xr, ylo)))

    to_y.wait_recv()
    fwd = piece(q_y, dp_core, 2)
    fwd.start()
    to_c.wait_recv()
    fwd.wait_recv()
    for i in range(4):
        pf[i] = pbuf[i].astype(F32)
    for t in range(TILES + 2):
        for i in range(4):
            mf[t, 20 * i:20 * i + 20, :] = pf[i, 20 * t:20 * t + 20, :]
    wbuf[z] = mf[0:TILES].astype(BF16)

    def ring(c, s):
        t0, n = CT * c, CT
        slot = (z - sgn * (s - 1) + 2 * NZ) % NZ
        ref = wbuf.at[slot, pl.ds(t0, n)]
        return rcopy(ref, ref, r_send.at[c, s - 1], r_recv.at[c, s - 1], (z_next, chan))

    def across(c, s):
        t0, n = CT * c, CT
        slot = (z - sgn * s + 2 * NZ) % NZ
        ref = wbuf.at[slot, pl.ds(t0, n)]
        return rcopy(ref, ref, c_send.at[c, s - 1], c_recv.at[c, s - 1], (dp_core, chan))

    def across_in(c, s):
        t0, n = CT * c, CT
        slot = (z + sgn * s + 2 * NZ) % NZ
        ref = wbuf.at[slot, pl.ds(t0, n)]
        return rcopy(ref, ref, c_send.at[c, s - 1], c_recv.at[c, s - 1], (dp_core, chan))

    def ring_in(c, s):
        t0, n = CT * c, CT
        slot = (z - sgn * s + 2 * NZ) % NZ
        ref = wbuf.at[slot, pl.ds(t0, n)]
        return rcopy(ref, ref, r_send.at[c, s - 1], r_recv.at[c, s - 1], (z_next, chan))

    def last_side(c):
        return core == (1 if c >= NC // 2 else 0)

    for c in range(NC):
        ring(c, 1).start()

    def ring_last(c):
        t0, n = CT * c, CT
        ref = wbuf.at[(z - sgn * 6 + 2 * NZ) % NZ, pl.ds(t0, n)]
        return rcopy(ref, ref, r_send.at[c, 7], r_recv.at[c, 7], (z_skip, chan))

    def ring_step(c, s):
        def body():
            ring_in(c, s).wait_recv()
            across(c, s).start()
        if s < 8:
            ring_in(c, s).wait_recv()
            if s < 7:
                ring(c, s + 1).start()
            if s == 6:
                pl.when(last_side(c))(lambda: ring_last(c).start())
            across(c, s).start()
        else:
            pl.when(last_side(c))(body)

    row0 = pl.multiple_of((80 * z) % 128, 16)
    e_w[pl.ds(row0, SLOT), 0:128] = mf[TILES].astype(BF16)
    e_w[pl.ds(row0, SLOT), 128:256] = mf[TILES + 1].astype(BF16)
    for k in range(1, NZ):
        emb_in(k).wait_recv()
    e_part[...] = jnp.dot(
        e_act[...].reshape(NZ, 256).astype(BF16), e_w[...],
        preferred_element_type=F32).reshape(NZ, 1, 256)
    e_sum[z] = e_part[z]
    for k in range(1, NZ):
        part_copy(k).start()

    def stats():
        def total(lo, n, centre):
            def step(k, acc):
                v = hown[pl.ds(pl.multiple_of(lo + 128 * k, 128), 128), :].astype(F32)
                if centre is not None:
                    v = v - centre
                    v = v * v
                return acc + jnp.sum(v.reshape(16, 8, 128), axis=0)
            acc = lax.fori_loop(0, n, step, jnp.zeros((8, 128), F32))
            return jnp.sum(acc, axis=0, keepdims=True)

        def fold(v):
            v = v + pltpu.roll(v, 64, 1)
            return v + pltpu.roll(v, 32, 1)

        def fold1(v):
            return fold(jnp.broadcast_to(v, (8, 128)))[0:1, :]

        m_main = total(0, 8, None) * (1.0 / 1024.0)
        m_res = fold1(total(1024, 2, None)) * (1.0 / 1024.0)
        v_main = total(0, 8, m_main) * (1.0 / 1024.0)
        v_res = fold1(total(1024, 2, m_res)) * (1.0 / 1024.0)
        return m_main, m_res, v_main, v_res, fold1

    m_main, m_res, v_main, v_res, fold1 = stats()

    def affine():
        for k in range(1, NZ):
            part_in(k).wait_recv()
        prod = jnp.sum(e_sum[...], axis=0)
        lane = lane_iota(1)
        prm = prm_ref[...]
        prm_res = jnp.concatenate([prm[:, 128:160]] * 4, axis=1)
        s_main = prod[0:1, 0:128] + prm[0:1, 0:128]
        s_res = fold1(jnp.where(lane < 32, prod[0:1, 128:256], 0.0)) + prm_res[0:1]
        u_main = m_main + s_main
        u_res = m_res + s_res

        def group(main, res):
            out_main = jnp.zeros((1, 128), F32)
            for g in range(3):
                inside = (lane >= 40 * g) & (lane < 40 * g + 40)
                t = jnp.sum(jnp.where(inside, main, 0.0), axis=1, keepdims=True) * (1.0 / 40.0)
                out_main = jnp.where(inside, t, out_main)
            t = jnp.sum(jnp.where(lane >= 120, main, 0.0) + jnp.where(lane < 32, res, 0.0),
                        axis=1, keepdims=True) * (1.0 / 40.0)
            return jnp.where(lane >= 120, t, out_main), jnp.broadcast_to(t, (1, 128))

        mean_main, mean_res = group(u_main, u_res)
        d_main = u_main - mean_main
        d_res = u_res - mean_res
        var_main, var_res = group(v_main + d_main * d_main, v_res + d_res * d_res)
        a_main = prm[1:2, 0:128] * lax.rsqrt(var_main + 1e-5)
        a_res = prm_res[1:2] * lax.rsqrt(var_res + 1e-5)
        b_main = prm[2:3, 0:128] + (s_main - mean_main) * a_main
        b_res = prm_res[2:3] + (s_res - mean_res) * a_res
        abv[me] = jnp.concatenate(
            [a_main, b_main, a_res, b_res, jnp.zeros((4, 128), F32)], axis=0)

    def ab_copy(k):
        return rcopy(abv.at[me], abv.at[me], b_send.at[k - 1], b_recv.at[k - 1], (dp, (chan + k) % 8))

    def ab_in(k):
        slot = (chan - k + 8) % 8
        return rcopy(abv.at[slot], abv.at[slot], b_send.at[k - 1], b_recv.at[k - 1], (dp, (chan + k) % 8))

    def normalise(src, slot):
        ab = abv[slot]

        def silu(v, a, b):
            v = v.astype(F32) * a + b
            half = 0.5 * v
            return half + half * jnp.tanh(half)

        lanes = pl.ds(pl.multiple_of(slot * 128, 128), 128)

        def step(k, carry):
            rows = pl.ds(pl.multiple_of(128 * k, 128), 128)
            nt[rows, lanes] = silu(src[rows, :], ab[0:1], ab[1:2]).astype(BF16)
            return carry
        lax.fori_loop(0, 8, step, 0)

        def step_res(k, carry):
            rows = pl.ds(pl.multiple_of(1024 + 128 * k, 128), 128)
            sbuf[slot, pl.ds(pl.multiple_of(128 * k, 128), 128), :] = silu(src[rows, :], ab[2:3], ab[3:4])
            return carry
        lax.fori_loop(0, 2, step_res, 0)

    def merge_tails():
        lane = lane_iota(256)
        for k in range(4):
            for half in range(2):
                acc = jnp.zeros((256, 128), F32)
                for m in range(4):
                    v = sbuf[4 * half + m]
                    shift = (32 * (m - k)) % 128
                    if shift:
                        v = pltpu.roll(v, shift, 1)
                    acc = jnp.where((lane >= 32 * m) & (lane < 32 * m + 32), v, acc)
                nt[256 * k:256 * k + 256, 1024 + 128 * half:1152 + 128 * half] = acc.astype(BF16)

    def place(slot, c):
        t0, n = CT * c, CT
        j = slot // 2
        odd = slot % 2
        lo = pl.multiple_of(128 * j + 80 * odd, 16)
        hi = pl.multiple_of((1 - odd) * (128 * j + 48) + odd * (1024 + 32 * j), 16)
        for t in range(t0, t0 + n):
            cols = slice(128 * t, 128 * t + 128)
            wk[pl.ds(lo, 48), cols] = wbuf[slot, t, 0:48, :]
            wk[pl.ds(hi, 32), cols] = wbuf[slot, t, 48:80, :]

    def place_all(s):
        for side in (-1, 1):
            slot = (z + side * sgn * s + 2 * NZ) % NZ
            for c in range(NC):
                place(slot, c)

    def across_wait(c, s):
        if s < 8:
            across_in(c, s).wait_recv()
        else:
            pl.when(core == (0 if c >= NC // 2 else 1))(lambda: across_in(c, s).wait_recv())

    xlb, xrb, yb_, ob = ch(xl, ylo), ch(xr, ylo), ch(x, yb), ch(xo, ylo)
    lyb, ryb, oyb = ch(xl, yb), ch(xr, yb), ch(xo, yb)

    for c in range(NC):
        place(z, c)

    for s in range(1, 9):
        for c in range(NC):
            ring_step(c, s)
        if s == 1:
            got(xlb, 0, 0).wait_recv()
            go(act(abuf.at[xlb], xlb, 0, ch(xr, ylo), 6))
            got(xrb, 1, 3).wait_recv()
            go(act(abuf.at[xrb], xrb, 1, ch(xl, ylo), 7))
            got(yb_, 0, 4).wait_recv()
            go(act(abuf.at[yb_], yb_, 0, ch(xr, ylo), 8))
            go(act(abuf.at[yb_], yb_, 0, ch(xl, ylo), 10))
            affine()
            for k in range(1, 8):
                ab_copy(k).start()
        if s == 2:
            got(yb_, 1, 5).wait_recv()
            go(act(abuf.at[yb_], yb_, 1, ch(xr, ylo), 9))
            go(act(abuf.at[yb_], yb_, 1, ch(xl, ylo), 11))
            normalise(hown, me)
        if s == 3:
            got(ob, 0, 6).wait_recv()
            go(act(abuf.at[ob], ob, 0, ch(x, yb), 12))
            got(ob, 1, 7).wait_recv()
            go(act(abuf.at[ob], ob, 1, ch(x, yb), 13))
            for k in range(1, 8):
                ab_in(k).wait_recv()
            got(xlb, 1, 1).wait_recv()
            normalise(abuf.at[xlb], xlb)
        if s == 4:
            got(xrb, 0, 2).wait_recv()
            normalise(abuf.at[xrb], xrb)
            normalise(abuf.at[yb_], yb_)
        if s == 5:
            normalise(abuf.at[ob], ob)
            got(lyb, 0, 8).wait_recv()
            got(lyb, 1, 9).wait_recv()
            normalise(abuf.at[lyb], lyb)
        if s == 6:
            got(ryb, 0, 10).wait_recv()
            got(ryb, 1, 11).wait_recv()
            normalise(abuf.at[ryb], ryb)
            got(oyb, 0, 12).wait_recv()
            got(oyb, 1, 13).wait_recv()
            normalise(abuf.at[oyb], oyb)
            merge_tails()
        if s > 1:
            for c in range(NC):
                across_wait(c, s - 1)
            place_all(s - 1)
    for c in range(NC):
        across_wait(c, 8)
        place((z + 8) % NZ, c)

    z_ref[0:PAD, :] = jnp.zeros((PAD, 1536), F32)
    z_ref[PAD + 1024:PAD + 1024 + PAD, :] = jnp.zeros((PAD, 1536), F32)

    def mm(n, carry):
        cols = pl.ds(pl.multiple_of(256 * n, 256), 256)
        z_ref[PAD:PAD + 1024, cols] = jnp.dot(nt[...], wk[:, cols], preferred_element_type=F32)
        return carry
    lax.fori_loop(0, 6, mm, 0)

    loads[3].wait()
    bias_main = prm_ref[3:4, 0:128]
    bias_res = jnp.concatenate([prm_ref[3:4, 128:160]] + [jnp.zeros((1, 96), F32)], axis=1)
    row = lax.broadcasted_iota(jnp.int32, (128, 128), 0) % 32
    lane = lane_iota(128)
    for k in range(8):
        base = PAD + 128 * k

        def band(tile, off):
            return z_ref[base + off:base + off + 128, 128 * tile:128 * tile + 128]

        side = [jnp.zeros((128, 128), F32)] * 3
        for dx in range(3):
            for dy in range(3):
                side[dx] = side[dx] + band(3 + 3 * dy + dx, 32 * (dy - 1) + dx - 1)
        main = side[1] + jnp.where(row > 0, side[0], 0.0) + jnp.where(row < 31, side[2], 0.0)
        res = [sum(band(dy, 32 * (dy - 1) + off) for dy in range(3)) for off in (-1, 0, 1)]
        u = jnp.where(lane < 32, jnp.where(row > 0, res[0], 0.0),
                      jnp.where(lane < 64, res[1],
                                jnp.where((lane < 96) & (row < 31), res[2], 0.0)))
        u = u + pltpu.roll(u, 96, 1) + pltpu.roll(u, 64, 1)
        cols = slice(128 * k, 128 * k + 128)
        out_ref[0:128, cols] = (skip_ref[0:128, cols].astype(F32) + (main + bias_main).T).astype(BF16)
        tail = (u + bias_res).T
        out_ref[128:160, cols] = (skip_ref[128:160, cols].astype(F32) + tail[0:32, :]).astype(BF16)

    to_y.wait_send()
    to_c.wait_send()
    fwd.wait_send()
    for copy in sent:
        copy.wait_send()
    for k in range(1, 8):
        ab_copy(k).wait_send()
    for k in range(1, NZ):
        emb_copy(k).wait_send()
        part_copy(k).wait_send()
    for c in range(NC):
        for s in range(1, 8):
            ring(c, s).wait_send()
            across(c, s).wait_send()

        @pl.when(last_side(c))
        def _():
            ring_last(c).wait_send()
            across(c, 8).wait_send()


def body(h_in, skip, emb, w_emb, b_emb, gn_gain, gn_bias, w_conv, b_conv):
    prm = jnp.stack([b_emb, gn_gain, gn_bias, b_conv])
    vmem = pl.BlockSpec(memory_space=pltpu.VMEM)
    hbm = pl.BlockSpec(memory_space=pltpu.MemorySpace.HBM)
    dma = pltpu.SemaphoreType.DMA
    out = pl.pallas_call(
        kernel,
        out_shape=jax.ShapeDtypeStruct((160, 1024), BF16),
        in_specs=[hbm, hbm, vmem, hbm, vmem, hbm],
        out_specs=vmem,
        scratch_shapes=[
            pltpu.VMEM((160, 1024), BF16),
            pltpu.VMEM((160, 1024), BF16),
            pltpu.VMEM((20, 160), BF16),
            pltpu.VMEM((9, 20, 160), BF16),
            pltpu.VMEM((ROWS, 128), BF16),
            pltpu.VMEM((4, PIECE, 128), BF16),
            pltpu.VMEM((4, PIECE, 128), F32),
            pltpu.VMEM((TILES + 2, SLOT, 128), F32),
            pltpu.VMEM((NZ, TILES, SLOT, 128), BF16),
            pltpu.VMEM((1280, 1536), BF16),
            pltpu.VMEM((8, ROWS, 128), BF16),
            pltpu.VMEM((1024, 1280), BF16),
            pltpu.VMEM((8, 256, 128), F32),
            pltpu.VMEM((8, 8, 128), F32),
            pltpu.VMEM((1024 + 2 * PAD, 1536), F32),
            pltpu.VMEM((1, 1408), F32),
            pltpu.VMEM((NZ, 1, 256), F32),
            pltpu.VMEM((256, 256), BF16),
            pltpu.VMEM((NZ, 1, 256), F32),
            pltpu.VMEM((NZ, 1, 256), F32),
            dma((4,)),
            dma((3,)), dma((3,)),
            dma((NC, 8)), dma((NC, 8)),
            dma((NC, 8)), dma((NC, 8)),
            dma((14,)), dma((14,)),
            dma((7,)), dma((7,)),
            dma((15,)), dma((15,)), dma((15,)), dma((15,)),
        ],
        compiler_params=pltpu.CompilerParams(
            collective_id=0, has_side_effects=True, vmem_limit_bytes=52 << 20),
        name="resblock",
    )(h_in, skip, emb, w_emb, prm, w_conv)
    return out[None]


def solution(mesh):
    return jax.shard_map(
        body,
        mesh=mesh,
        in_specs=(
            P("dp", "chan", None),
            P("dp", "chan", None),
            P("dp", None),
            P("dp", "chan"),
            P("chan"),
            P("chan"),
            P("chan"),
            P(None, "dp", "chan"),
            P("chan"),
        ),
        out_specs=P("dp", "chan", None),
        check_vma=False,
    )
```

```python
import jax
import jax.numpy as jnp
from jax import lax
from jax.experimental import pallas as pl
from jax.experimental.pallas import tpu as pltpu
from jax.sharding import PartitionSpec as P

MESH = pl.DeviceIdType.MESH
F32 = jnp.float32
BF16 = jnp.bfloat16

NZ = 16
TILES = 12
SLOT = 80
PIECE = 240
EP = 48
CUT = (0, 128, 240)
ROWS = 1280
HALF = 640
PAD = 40


def lane_iota(rows):
    return lax.broadcasted_iota(jnp.int32, (rows, 128), 1)


def kernel(
    h_hbm, skip_hbm, emb_ref, wemb_hbm, b_emb_ref, gain_ref, bias_ref, b_conv_ref, w_hbm, out_ref,
    h_ref, skip_ref, wemb_ref, w_ref,
    hown, pbuf, pf, mf, ep, ef, em, wk, abuf, nt, sbuf, abv, z_ref,
    actv, e_act, e_w, e_part, e_sum,
    in_sem, y_send, y_recv, o_send, o_recv, r_send, r_recv, c_send, c_recv,
    a_send, a_recv, b_send, b_recv, e_send, e_recv, f_send, f_recv,
):
    dp = lax.axis_index("dp")
    chan = lax.axis_index("chan")
    z = dp // 4
    yhi = (dp // 2) % 2
    core = dp % 2
    sgn = 1 - 2 * core
    x = chan // 2
    ylo = chan % 2

    loads = [
        pltpu.make_async_copy(w_hbm, w_ref, in_sem.at[0]),
        pltpu.make_async_copy(wemb_hbm, wemb_ref, in_sem.at[1]),
        pltpu.make_async_copy(h_hbm.at[0], h_ref, in_sem.at[2]),
        pltpu.make_async_copy(skip_hbm.at[0], skip_ref, in_sem.at[3]),
    ]
    for load in loads:
        load.start()

    def dp_at(zz, yy, cc):
        return zz * 4 + yy * 2 + cc

    dp_core = dp_at(z, yhi, 1 - core)
    dp_yhi = dp_at(z, 1 - yhi, core)
    xr = (x + 1) % 4
    xl = (x + 3) % 4
    xo = (x + 2) % 4
    yb = 1 - ylo

    def ch(xx, yy):
        return xx * 2 + yy

    barrier = pltpu.get_barrier_semaphore()
    for d in [dp_core, dp_yhi] + [dp_at((z + k) % NZ, yhi, core) for k in range(1, NZ)]:
        pl.semaphore_signal(barrier, inc=1, device_id=(d, chan), device_id_type=MESH)
    for k in range(1, 8):
        pl.semaphore_signal(barrier, inc=1, device_id=(dp, (chan + k) % 8), device_id_type=MESH)

    def rcopy(src, dst, ssem, rsem, dev):
        return pltpu.make_async_remote_copy(
            src_ref=src, dst_ref=dst, send_sem=ssem, recv_sem=rsem,
            device_id=dev, device_id_type=MESH,
        )

    q = 2 * yhi + core
    ef[0, 32:48, :] = jnp.zeros((16, 128), F32)
    loads[0].wait()
    loads[1].wait()
    for dy in range(3):
        taps = [w_ref[3 * dy + dx].astype(F32) for dx in range(3)]
        pf[0, 20 * dy:20 * dy + 20, :] = jnp.concatenate(
            [t[:, 128:160] for t in taps] + [jnp.zeros((20, 32), F32)], axis=1)
        for dx in range(3):
            t = 3 + 3 * dy + dx
            pf[0, 20 * t:20 * t + 20, :] = taps[dx][:, 0:128]
    emb_w = wemb_ref[...].astype(F32)
    ef[0, 0:20, :] = emb_w[:, 0:128]
    ef[0, 20:40, :] = jnp.concatenate([emb_w[:, 128:160], jnp.zeros((20, 96), F32)], axis=1)
    pbuf[z, q] = pf[0].astype(BF16)
    ep[q] = ef[0].astype(BF16)

    e = emb_ref[...].astype(F32)
    actv[:, 0:1280] = (e / (1.0 + jnp.exp(-e))).astype(BF16).astype(F32)
    actv[:, 1280:1408] = jnp.zeros((1, 128), F32)

    def window(zz):
        return pl.ds(pl.multiple_of(128 * ((80 * zz) // 128), 128), 256)

    e_act[z] = actv[:, window(z)]
    e_w[...] = jnp.zeros((256, 256), BF16)
    z_ref[0:PAD, :] = jnp.zeros((PAD, 1536), F32)
    z_ref[PAD + 1024:PAD + 1024 + PAD, :] = jnp.zeros((PAD, 1536), F32)

    loads[2].wait()
    for k in range(8):
        blk = h_ref[0:128, 128 * k:128 * k + 128].astype(F32)
        hown[128 * k:128 * k + 128, :] = blk.T.astype(BF16)
    for k in range(2):
        blk = jnp.concatenate(
            [h_ref[128:160, 256 * m + 128 * k:256 * m + 128 * k + 128] for m in range(4)],
            axis=0).astype(F32)
        hown[1024 + 128 * k:1024 + 128 * k + 128, :] = blk.T.astype(BF16)

    pl.semaphore_wait(barrier, 24)

    mine, peer = core, 1 - core

    def piece_at(r, k):
        return 2 * (yhi if r == 0 else 1 - yhi) + k

    def part(slot, qq, c):
        return pbuf.at[slot, qq, pl.ds(CUT[c], CUT[c + 1] - CUT[c])]

    def plane(side, s):
        return lax.rem(z - (sgn if side == 0 else -sgn) * s + NZ, NZ)

    def sem_at(r, k, c, s):
        return ((r * 2 + k) * 2 + c) * 8 + s - 1

    def ring(r, k, c, s):
        ref = part(plane(0, s - 1), piece_at(r, k), c)
        i = sem_at(r, k, c, s)
        return rcopy(ref, ref, r_send.at[i], r_recv.at[i], (dp_at(plane(1, 1), yhi, core), chan))

    def ring_last(r, c):
        ref = part(plane(0, 6), piece_at(r, mine), c)
        i = sem_at(r, mine, c, 8)
        return rcopy(ref, ref, r_send.at[i], r_recv.at[i], (dp_at(plane(1, 2), yhi, core), chan))

    def ring_in(r, k, c, s):
        ref = part(plane(0, s), piece_at(r, k), c)
        i = sem_at(r, k, c, s)
        return rcopy(ref, ref, r_send.at[i], r_recv.at[i], (dp_core, chan))

    def across(r, k, c, s):
        ref = part(plane(0, s), piece_at(r, k), c)
        i = sem_at(r, k, c, s)
        return rcopy(ref, ref, c_send.at[i], c_recv.at[i], (dp_core, chan))

    def across_in(r, k, c, s):
        ref = part(plane(1, s), piece_at(r, k), c)
        i = sem_at(r, k, c, s)
        return rcopy(ref, ref, c_send.at[i], c_recv.at[i], (dp_core, chan))

    qs = (piece_at(0, mine), piece_at(1, mine))
    qs_in = (piece_at(0, peer), piece_at(1, peer))

    def row_out(c):
        ref = part(z, qs[0], c) if c < 2 else ep.at[qs[0]]
        return rcopy(ref, ref, y_send.at[c], y_recv.at[c], (dp_yhi, chan))

    def row_in(c):
        ref = part(z, qs[1], c) if c < 2 else ep.at[qs[1]]
        return rcopy(ref, ref, y_send.at[c], y_recv.at[c], (dp_yhi, chan))

    def own_out(r, c):
        ref = part(z, qs[r], c) if c < 2 else ep.at[qs[r]]
        return rcopy(ref, ref, o_send.at[3 * r + c], o_recv.at[3 * r + c], (dp_core, chan))

    def own_in(r, c):
        ref = part(z, qs_in[r], c) if c < 2 else ep.at[qs_in[r]]
        return rcopy(ref, ref, o_send.at[3 * r + c], o_recv.at[3 * r + c], (dp_core, chan))

    for c in range(2):
        own_out(0, c).start()
        ring(0, mine, c, 1).start()
    row_out(2).start()
    for c in range(2):
        row_out(c).start()
    own_out(0, 2).start()
    for c in range(2):
        own_in(0, c).wait_recv()
        ring(0, peer, c, 1).start()

    def emb_copy(k):
        zz = (z + k) % NZ
        return rcopy(actv.at[:, window(zz)], e_act.at[z], e_send.at[k - 1], e_recv.at[k - 1], (dp_at(zz, yhi, core), chan))

    def emb_in(k):
        slot = (z - k + NZ) % NZ
        return rcopy(e_act.at[slot], e_act.at[slot], e_send.at[k - 1], e_recv.at[k - 1], (dp_core, chan))

    def part_copy(k):
        zz = (z + k) % NZ
        return rcopy(e_part.at[zz], e_sum.at[z], f_send.at[k - 1], f_recv.at[k - 1], (dp_at(zz, yhi, core), chan))

    def part_in(k):
        slot = (z - k + NZ) % NZ
        return rcopy(e_sum.at[slot], e_sum.at[slot], f_send.at[k - 1], f_recv.at[k - 1], (dp_core, chan))

    def act(src, slot, half, dev_chan, i):
        rows = pl.ds(HALF * half, HALF)
        return rcopy(src.at[rows, :], abuf.at[slot, rows, :], a_send.at[i], a_recv.at[i], (dp, dev_chan))

    sent = []
    me = ch(x, ylo)

    def go(copy):
        copy.start()
        sent.append(copy)

    go(act(hown, me, 0, ch(xr, ylo), 0))
    go(act(hown, me, 1, ch(xl, ylo), 3))
    go(act(hown, me, 0, ch(x, yb), 4))
    go(act(hown, me, 1, ch(xr, ylo), 1))
    go(act(hown, me, 0, ch(xl, ylo), 2))
    go(act(hown, me, 1, ch(x, yb), 5))

    for k in range(1, NZ):
        emb_copy(k).start()

    def got(slot, half, i):
        rows = pl.ds(HALF * half, HALF)
        return rcopy(abuf.at[slot, rows, :], abuf.at[slot, rows, :], a_send.at[i], a_recv.at[i], (dp, ch(xr, ylo)))

    def emb_step():
        for i in range(4):
            ef[i] = ep[i].astype(F32)
        for t in range(2):
            for i in range(4):
                em[t, 20 * i:20 * i + 20, :] = ef[i, 20 * t:20 * t + 20, :]
        row0 = pl.multiple_of((80 * z) % 128, 16)
        e_w[pl.ds(row0, SLOT), 0:128] = em[0].astype(BF16)
        e_w[pl.ds(row0, SLOT), 128:256] = em[1].astype(BF16)
        for k in range(1, NZ):
            emb_in(k).wait_recv()
        e_part[...] = jnp.dot(
            e_act[...].reshape(NZ, 256).astype(BF16), e_w[...],
            preferred_element_type=F32).reshape(NZ, 1, 256)
        e_sum[z] = e_part[z]
        for k in range(1, NZ):
            part_copy(k).start()

    def stats():
        def total(lo, n, centre):
            def step(k, acc):
                v = hown[pl.ds(pl.multiple_of(lo + 128 * k, 128), 128), :].astype(F32)
                if centre is not None:
                    v = v - centre
                    v = v * v
                return acc + jnp.sum(v.reshape(16, 8, 128), axis=0)
            acc = lax.fori_loop(0, n, step, jnp.zeros((8, 128), F32))
            return jnp.sum(acc, axis=0, keepdims=True)

        def fold(v):
            v = v + pltpu.roll(v, 64, 1)
            return v + pltpu.roll(v, 32, 1)

        def fold1(v):
            return fold(jnp.broadcast_to(v, (8, 128)))[0:1, :]

        m_main = total(0, 8, None) * (1.0 / 1024.0)
        m_res = fold1(total(1024, 2, None)) * (1.0 / 1024.0)
        v_main = total(0, 8, m_main) * (1.0 / 1024.0)
        v_res = fold1(total(1024, 2, m_res)) * (1.0 / 1024.0)
        return m_main, m_res, v_main, v_res, fold1

    def affine(m_main, m_res, v_main, v_res, fold1):
        for k in range(1, NZ):
            part_in(k).wait_recv()
        prod = jnp.sum(e_sum[...], axis=0)
        lane = lane_iota(1)
        prm = jnp.concatenate([b_emb_ref[...], gain_ref[...], bias_ref[...]], axis=0)
        prm_res = jnp.concatenate([prm[:, 128:160]] * 4, axis=1)
        s_main = prod[0:1, 0:128] + prm[0:1, 0:128]
        s_res = fold1(jnp.where(lane < 32, prod[0:1, 128:256], 0.0)) + prm_res[0:1]
        u_main = m_main + s_main
        u_res = m_res + s_res

        def group(main, res):
            out_main = jnp.zeros((1, 128), F32)
            for g in range(3):
                inside = (lane >= 40 * g) & (lane < 40 * g + 40)
                t = jnp.sum(jnp.where(inside, main, 0.0), axis=1, keepdims=True) * (1.0 / 40.0)
                out_main = jnp.where(inside, t, out_main)
            t = jnp.sum(jnp.where(lane >= 120, main, 0.0) + jnp.where(lane < 32, res, 0.0),
                        axis=1, keepdims=True) * (1.0 / 40.0)
            return jnp.where(lane >= 120, t, out_main), jnp.broadcast_to(t, (1, 128))

        mean_main, mean_res = group(u_main, u_res)
        d_main = u_main - mean_main
        d_res = u_res - mean_res
        var_main, var_res = group(v_main + d_main * d_main, v_res + d_res * d_res)
        a_main = prm[1:2, 0:128] * lax.rsqrt(var_main + 1e-5)
        a_res = prm_res[1:2] * lax.rsqrt(var_res + 1e-5)
        b_main = prm[2:3, 0:128] + (s_main - mean_main) * a_main
        b_res = prm_res[2:3] + (s_res - mean_res) * a_res
        abv[me] = jnp.concatenate(
            [a_main, b_main, a_res, b_res, jnp.zeros((4, 128), F32)], axis=0)

    def ab_copy(k):
        return rcopy(abv.at[me], abv.at[me], b_send.at[k - 1], b_recv.at[k - 1], (dp, (chan + k) % 8))

    def ab_in(k):
        slot = (chan - k + 8) % 8
        return rcopy(abv.at[slot], abv.at[slot], b_send.at[k - 1], b_recv.at[k - 1], (dp, (chan + k) % 8))

    def normalise(src, slot):
        ab = abv[slot]

        def silu(v, a, b):
            v = v.astype(F32) * a + b
            half = 0.5 * v
            return half + half * jnp.tanh(half)

        lanes = pl.ds(pl.multiple_of(slot * 128, 128), 128)

        def step(k, carry):
            rows = pl.ds(pl.multiple_of(128 * k, 128), 128)
            nt[rows, lanes] = silu(src[rows, :], ab[0:1], ab[1:2]).astype(BF16)
            return carry
        lax.fori_loop(0, 8, step, 0)

        def step_res(k, carry):
            rows = pl.ds(pl.multiple_of(1024 + 128 * k, 128), 128)
            sbuf[slot, pl.ds(pl.multiple_of(128 * k, 128), 128), :] = silu(src[rows, :], ab[2:3], ab[3:4])
            return carry
        lax.fori_loop(0, 2, step_res, 0)

    def merge_tails():
        lane = lane_iota(256)
        for k in range(4):
            for half in range(2):
                acc = jnp.zeros((256, 128), F32)
                for m in range(4):
                    v = sbuf[4 * half + m]
                    shift = (32 * (m - k)) % 128
                    if shift:
                        v = pltpu.roll(v, shift, 1)
                    acc = jnp.where((lane >= 32 * m) & (lane < 32 * m + 32), v, acc)
                nt[256 * k:256 * k + 256, 1024 + 128 * half:1152 + 128 * half] = acc.astype(BF16)

    def place(slot):
        for i in range(4):
            pf[i] = pbuf[slot, i].astype(F32)
        for t in range(TILES):
            for i in range(4):
                mf[t, 20 * i:20 * i + 20, :] = pf[i, 20 * t:20 * t + 20, :]
        j = lax.div(slot, 2)
        odd = lax.rem(slot, 2)
        main = 128 * j
        lo = pl.multiple_of(main + 80 * odd, 16)
        hi = pl.multiple_of((1 - odd) * (main + 48) + odd * (1024 + 32 * j), 16)
        for t in range(TILES):
            cols = slice(128 * t, 128 * t + 128)
            wk[pl.ds(lo, 48), cols] = mf[t, 0:48, :].astype(BF16)
            wk[pl.ds(hi, 32), cols] = mf[t, 48:80, :].astype(BF16)

    xlb, xrb, yb_, ob = ch(xl, ylo), ch(xr, ylo), ch(x, yb), ch(xo, ylo)
    lyb, ryb, oyb = ch(xl, yb), ch(xr, yb), ch(xo, yb)

    def arrive(r, s):
        for k in (mine, peer):
            for c in range(2):
                ring_in(r, k, c, s).wait_recv()
                if s < 7:
                    ring(r, k, c, s + 1).start()
                across(r, k, c, s).start()
        if s == 6:
            for c in range(2):
                ring_last(r, c).start()
        if s == 7:
            for c in range(2):
                ring_in(r, mine, c, 8).wait_recv()
                across(r, mine, c, 8).start()

    def settle(s):
        for r in range(2):
            for k in (peer, mine):
                for c in range(2):
                    across_in(r, k, c, s).wait_recv()
        for side in range(2):
            place(plane(side, s))

    for s in range(1, 9):
        if s <= 7:
            arrive(0, s)
        if s == 1:
            for c in range(2):
                row_in(c).wait_recv()
                ring(1, mine, c, 1).start()
                own_out(1, c).start()
            row_in(2).wait_recv()
            own_out(1, 2).start()
            for c in range(2):
                own_in(1, c).wait_recv()
                ring(1, peer, c, 1).start()
        else:
            arrive(1, s - 1)
        if s == 1:
            own_in(0, 2).wait_recv()
            own_in(1, 2).wait_recv()
            emb_step()
        if s == 2:
            got(xlb, 0, 0).wait_recv()
            go(act(abuf.at[xlb], xlb, 0, ch(xr, ylo), 6))
            got(xrb, 1, 3).wait_recv()
            go(act(abuf.at[xrb], xrb, 1, ch(xl, ylo), 7))
            got(yb_, 0, 4).wait_recv()
            go(act(abuf.at[yb_], yb_, 0, ch(xr, ylo), 8))
            go(act(abuf.at[yb_], yb_, 0, ch(xl, ylo), 10))
            moments = stats()
        if s == 3:
            got(yb_, 1, 5).wait_recv()
            go(act(abuf.at[yb_], yb_, 1, ch(xr, ylo), 9))
            go(act(abuf.at[yb_], yb_, 1, ch(xl, ylo), 11))
            affine(*moments)
            for k in range(1, 8):
                ab_copy(k).start()
            place(z)
            settle(1)
        if s == 4:
            got(ob, 0, 6).wait_recv()
            go(act(abuf.at[ob], ob, 0, ch(x, yb), 12))
            got(ob, 1, 7).wait_recv()
            go(act(abuf.at[ob], ob, 1, ch(x, yb), 13))
            settle(2)
            normalise(hown, me)
            settle(3)
        if s == 5:
            for k in range(1, 8):
                ab_in(k).wait_recv()
            got(xlb, 1, 1).wait_recv()
            normalise(abuf.at[xlb], xlb)
            got(xrb, 0, 2).wait_recv()
            normalise(abuf.at[xrb], xrb)
            normalise(abuf.at[yb_], yb_)
            settle(4)
        if s == 6:
            normalise(abuf.at[ob], ob)
            got(lyb, 0, 8).wait_recv()
            got(lyb, 1, 9).wait_recv()
            normalise(abuf.at[lyb], lyb)
            got(ryb, 0, 10).wait_recv()
            got(ryb, 1, 11).wait_recv()
            normalise(abuf.at[ryb], ryb)
            settle(5)
        if s == 7:
            got(oyb, 0, 12).wait_recv()
            got(oyb, 1, 13).wait_recv()
            normalise(abuf.at[oyb], oyb)
            settle(6)
            merge_tails()
    settle(7)
    for r in range(2):
        for c in range(2):
            across_in(r, peer, c, 8).wait_recv()
    place(plane(0, 8))


    def product(n, carry):
        cols = pl.ds(pl.multiple_of(256 * n, 256), 256)
        z_ref[PAD:PAD + 1024, cols] = jnp.dot(nt[...], wk[:, cols], preferred_element_type=F32)
        return carry
    lax.fori_loop(0, 6, product, 0)

    loads[3].wait()
    bias_main = b_conv_ref[:, 0:128]
    bias_res = jnp.concatenate([b_conv_ref[:, 128:160]] + [jnp.zeros((1, 96), F32)], axis=1)
    row = lax.broadcasted_iota(jnp.int32, (128, 128), 0) % 32
    lane = lane_iota(128)
    for k in range(8):
        base = PAD + 128 * k

        def band(tile, off):
            return z_ref[base + off:base + off + 128, 128 * tile:128 * tile + 128]

        side = [jnp.zeros((128, 128), F32)] * 3
        for dx in range(3):
            for dy in range(3):
                side[dx] = side[dx] + band(3 + 3 * dy + dx, 32 * (dy - 1) + dx - 1)
        main = side[1] + jnp.where(row > 0, side[0], 0.0) + jnp.where(row < 31, side[2], 0.0)
        res = [sum(band(dy, 32 * (dy - 1) + off) for dy in range(3)) for off in (-1, 0, 1)]
        u = jnp.where(lane < 32, jnp.where(row > 0, res[0], 0.0),
                      jnp.where(lane < 64, res[1],
                                jnp.where((lane < 96) & (row < 31), res[2], 0.0)))
        u = u + pltpu.roll(u, 96, 1) + pltpu.roll(u, 64, 1)
        cols = slice(128 * k, 128 * k + 128)
        out_ref[0:128, cols] = (skip_ref[0:128, cols].astype(F32) + (main + bias_main).T).astype(BF16)
        tail = (u + bias_res).T
        out_ref[128:160, cols] = (skip_ref[128:160, cols].astype(F32) + tail[0:32, :]).astype(BF16)

    for c in range(3):
        row_out(c).wait_send()
        own_out(0, c).wait_send()
        own_out(1, c).wait_send()
    for copy in sent:
        copy.wait_send()
    for k in range(1, 8):
        ab_copy(k).wait_send()
    for k in range(1, NZ):
        emb_copy(k).wait_send()
        part_copy(k).wait_send()
    for r in range(2):
        for c in range(2):
            for k in (mine, peer):
                for s in range(1, 8):
                    ring(r, k, c, s).wait_send()
                    across(r, k, c, s).wait_send()
            ring_last(r, c).wait_send()
            across(r, mine, c, 8).wait_send()


def body(h_in, skip, emb, w_emb, b_emb, gn_gain, gn_bias, w_conv, b_conv):
    rows = [v[None] for v in (b_emb, gn_gain, gn_bias, b_conv)]
    vmem = pl.BlockSpec(memory_space=pltpu.VMEM)
    hbm = pl.BlockSpec(memory_space=pltpu.MemorySpace.HBM)
    dma = pltpu.SemaphoreType.DMA
    out = pl.pallas_call(
        kernel,
        out_shape=jax.ShapeDtypeStruct((160, 1024), BF16),
        in_specs=[hbm, hbm, vmem, hbm, vmem, vmem, vmem, vmem, hbm],
        out_specs=vmem,
        scratch_shapes=[
            pltpu.VMEM((160, 1024), BF16),
            pltpu.VMEM((160, 1024), BF16),
            pltpu.VMEM((20, 160), BF16),
            pltpu.VMEM((9, 20, 160), BF16),
            pltpu.VMEM((ROWS, 128), BF16),
            pltpu.VMEM((NZ, 4, PIECE, 128), BF16),
            pltpu.VMEM((4, PIECE, 128), F32),
            pltpu.VMEM((TILES, SLOT, 128), F32),
            pltpu.VMEM((4, EP, 128), BF16),
            pltpu.VMEM((4, EP, 128), F32),
            pltpu.VMEM((2, SLOT, 128), F32),
            pltpu.VMEM((1280, 1536), BF16),
            pltpu.VMEM((8, ROWS, 128), BF16),
            pltpu.VMEM((1024, 1280), BF16),
            pltpu.VMEM((8, 256, 128), F32),
            pltpu.VMEM((8, 8, 128), F32),
            pltpu.VMEM((1024 + 2 * PAD, 1536), F32),
            pltpu.VMEM((1, 1408), F32),
            pltpu.VMEM((NZ, 1, 256), F32),
            pltpu.VMEM((256, 256), BF16),
            pltpu.VMEM((NZ, 1, 256), F32),
            pltpu.VMEM((NZ, 1, 256), F32),
            dma((4,)),
            dma((3,)), dma((3,)), dma((6,)), dma((6,)),
            dma((64,)), dma((64,)), dma((64,)), dma((64,)),
            dma((14,)), dma((14,)),
            dma((7,)), dma((7,)),
            dma((15,)), dma((15,)), dma((15,)), dma((15,)),
        ],
        compiler_params=pltpu.CompilerParams(
            collective_id=0, has_side_effects=True, vmem_limit_bytes=56 << 20),
        name="resblock",
    )(h_in, skip, emb, w_emb, *rows, w_conv)
    return out[None]


def solution(mesh):
    return jax.shard_map(
        body,
        mesh=mesh,
        in_specs=(
            P("dp", "chan", None),
            P("dp", "chan", None),
            P("dp", None),
            P("dp", "chan"),
            P("chan"),
            P("chan"),
            P("chan"),
            P(None, "dp", "chan"),
            P("chan"),
        ),
        out_specs=P("dp", "chan", None),
        check_vma=False,
    )
```

```python
import jax
import jax.numpy as jnp
from jax import lax
from jax.experimental import pallas as pl
from jax.experimental.pallas import tpu as pltpu
from jax.sharding import PartitionSpec as P

MESH = pl.DeviceIdType.MESH
F32 = jnp.float32
BF16 = jnp.bfloat16

NZ = 16
TILES = 12
SLOT = 80
PIECE = 240
EP = 48
CUT = (0, 128, 240)
ROWS = 1280
HALF = 640
PAD = 40


def lane_iota(rows):
    return lax.broadcasted_iota(jnp.int32, (rows, 128), 1)


def kernel(
    h_hbm, skip_hbm, emb_ref, wemb_hbm, b_emb_ref, gain_ref, bias_ref, b_conv_ref, w_hbm, out_ref,
    h_ref, skip_ref, wemb_ref, w_ref,
    hown, pbuf, pf, mf, ep, ef, em, wk, abuf, nt, sbuf, abv, z_ref,
    actv, e_act, e_w, e_part, e_sum,
    in_sem, y_send, y_recv, o_send, o_recv, r_send, r_recv, c_send, c_recv,
    a_send, a_recv, b_send, b_recv, e_send, e_recv, f_send, f_recv,
):
    dp = lax.axis_index("dp")
    chan = lax.axis_index("chan")
    z = dp // 4
    yhi = (dp // 2) % 2
    core = dp % 2
    x = chan // 2
    ylo = chan % 2

    loads = [
        pltpu.make_async_copy(w_hbm, w_ref, in_sem.at[0]),
        pltpu.make_async_copy(wemb_hbm, wemb_ref, in_sem.at[1]),
        pltpu.make_async_copy(h_hbm.at[0], h_ref, in_sem.at[2]),
        pltpu.make_async_copy(skip_hbm.at[0], skip_ref, in_sem.at[3]),
    ]
    for load in loads:
        load.start()

    def dp_at(zz, yy, cc):
        return zz * 4 + yy * 2 + cc

    dp_core = dp_at(z, yhi, 1 - core)
    dp_yhi = dp_at(z, 1 - yhi, core)
    xr = (x + 1) % 4
    xl = (x + 3) % 4
    xo = (x + 2) % 4
    yb = 1 - ylo

    def ch(xx, yy):
        return xx * 2 + yy

    barrier = pltpu.get_barrier_semaphore()
    for d in [dp_core, dp_yhi] + [dp_at((z + k) % NZ, yhi, core) for k in range(1, NZ)]:
        pl.semaphore_signal(barrier, inc=1, device_id=(d, chan), device_id_type=MESH)
    for k in range(1, 8):
        pl.semaphore_signal(barrier, inc=1, device_id=(dp, (chan + k) % 8), device_id_type=MESH)

    def rcopy(src, dst, ssem, rsem, dev):
        return pltpu.make_async_remote_copy(
            src_ref=src, dst_ref=dst, send_sem=ssem, recv_sem=rsem,
            device_id=dev, device_id_type=MESH,
        )

    q = 2 * yhi + core
    ef[0, 32:48, :] = jnp.zeros((16, 128), F32)
    loads[0].wait()
    loads[1].wait()
    for dy in range(3):
        taps = [w_ref[3 * dy + dx].astype(F32) for dx in range(3)]
        pf[0, 20 * dy:20 * dy + 20, :] = jnp.concatenate(
            [t[:, 128:160] for t in taps] + [jnp.zeros((20, 32), F32)], axis=1)
        for dx in range(3):
            t = 3 + 3 * dy + dx
            pf[0, 20 * t:20 * t + 20, :] = taps[dx][:, 0:128]
    emb_w = wemb_ref[...].astype(F32)
    ef[0, 0:20, :] = emb_w[:, 0:128]
    ef[0, 20:40, :] = jnp.concatenate([emb_w[:, 128:160], jnp.zeros((20, 96), F32)], axis=1)
    pbuf[z, q] = pf[0].astype(BF16)
    ep[q] = ef[0].astype(BF16)

    e = emb_ref[...].astype(F32)
    actv[:, 0:1280] = (e / (1.0 + jnp.exp(-e))).astype(BF16).astype(F32)
    actv[:, 1280:1408] = jnp.zeros((1, 128), F32)

    def window(zz):
        return pl.ds(pl.multiple_of(128 * ((80 * zz) // 128), 128), 256)

    e_act[z] = actv[:, window(z)]
    e_w[...] = jnp.zeros((256, 256), BF16)

    pl.semaphore_wait(barrier, 24)

    qs = (q, 2 * (1 - yhi) + core)
    qs_in = (2 * yhi + (1 - core), 2 * (1 - yhi) + (1 - core))

    def part(slot, qq, c):
        return pbuf.at[slot, qq, pl.ds(CUT[c], CUT[c + 1] - CUT[c])]

    def plane(d, s):
        return lax.rem(z - s + NZ, NZ) if d == 0 else lax.rem(z + s, NZ)

    def sem_at(d, r, c, s):
        return ((d * 2 + r) * 2 + c) * 8 + s - 1

    def ring(d, r, c, s):
        ref = part(plane(d, s - 1), qs[r], c)
        i = sem_at(d, r, c, s)
        return rcopy(ref, ref, r_send.at[i], r_recv.at[i], (dp_at(plane(1 - d, 1), yhi, core), chan))

    def ring_last(d, c):
        ref = part(plane(d, 6), qs[d], c)
        i = sem_at(d, d, c, 8)
        return rcopy(ref, ref, r_send.at[i], r_recv.at[i], (dp_at(plane(1 - d, 2), yhi, core), chan))

    def ring_in(d, r, c, s):
        ref = part(plane(d, s), qs[r], c)
        i = sem_at(d, r, c, s)
        return rcopy(ref, ref, r_send.at[i], r_recv.at[i], (dp_core, chan))

    def across(d, r, c, s):
        ref = part(plane(d, s), qs[r], c)
        i = sem_at(d, r, c, s)
        return rcopy(ref, ref, c_send.at[i], c_recv.at[i], (dp_core, chan))

    def across_in(d, r, c, s):
        ref = part(plane(d, s), qs_in[r], c)
        i = sem_at(d, r, c, s)
        return rcopy(ref, ref, c_send.at[i], c_recv.at[i], (dp_core, chan))

    def row_out(c):
        ref = part(z, qs[0], c) if c < 2 else ep.at[qs[0]]
        return rcopy(ref, ref, y_send.at[c], y_recv.at[c], (dp_yhi, chan))

    def row_in(c):
        ref = part(z, qs[1], c) if c < 2 else ep.at[qs[1]]
        return rcopy(ref, ref, y_send.at[c], y_recv.at[c], (dp_yhi, chan))

    def own_out(r, c):
        ref = part(z, qs[r], c) if c < 2 else ep.at[qs[r]]
        return rcopy(ref, ref, o_send.at[3 * r + c], o_recv.at[3 * r + c], (dp_core, chan))

    def own_in(r, c):
        ref = part(z, qs_in[r], c) if c < 2 else ep.at[qs_in[r]]
        return rcopy(ref, ref, o_send.at[3 * r + c], o_recv.at[3 * r + c], (dp_core, chan))

    row_out(2).start()
    for c in range(2):
        for d in range(2):
            ring(d, 0, c, 1).start()
        row_out(c).start()
    for c in (2, 0, 1):
        own_out(0, c).start()

    def emb_copy(k):
        zz = (z + k) % NZ
        return rcopy(actv.at[:, window(zz)], e_act.at[z], e_send.at[k - 1], e_recv.at[k - 1], (dp_at(zz, yhi, core), chan))

    def emb_in(k):
        slot = (z - k + NZ) % NZ
        return rcopy(e_act.at[slot], e_act.at[slot], e_send.at[k - 1], e_recv.at[k - 1], (dp_core, chan))

    def part_copy(k):
        zz = (z + k) % NZ
        return rcopy(e_part.at[zz], e_sum.at[z], f_send.at[k - 1], f_recv.at[k - 1], (dp_at(zz, yhi, core), chan))

    def part_in(k):
        slot = (z - k + NZ) % NZ
        return rcopy(e_sum.at[slot], e_sum.at[slot], f_send.at[k - 1], f_recv.at[k - 1], (dp_core, chan))

    for k in range(1, NZ):
        emb_copy(k).start()

    loads[2].wait()
    for k in range(8):
        blk = h_ref[0:128, 128 * k:128 * k + 128].astype(F32)
        hown[128 * k:128 * k + 128, :] = blk.T.astype(BF16)
    for k in range(2):
        blk = jnp.concatenate(
            [h_ref[128:160, 256 * m + 128 * k:256 * m + 128 * k + 128] for m in range(4)],
            axis=0).astype(F32)
        hown[1024 + 128 * k:1024 + 128 * k + 128, :] = blk.T.astype(BF16)


    def act(src, slot, half, dev_chan, i):
        rows = pl.ds(HALF * half, HALF)
        return rcopy(src.at[rows, :], abuf.at[slot, rows, :], a_send.at[i], a_recv.at[i], (dp, dev_chan))

    sent = []
    me = ch(x, ylo)

    def go(copy):
        copy.start()
        sent.append(copy)

    go(act(hown, me, 0, ch(xr, ylo), 0))
    go(act(hown, me, 1, ch(xl, ylo), 3))
    go(act(hown, me, 0, ch(x, yb), 4))
    go(act(hown, me, 1, ch(xr, ylo), 1))
    go(act(hown, me, 0, ch(xl, ylo), 2))
    go(act(hown, me, 1, ch(x, yb), 5))

    def got(slot, half, i):
        rows = pl.ds(HALF * half, HALF)
        return rcopy(abuf.at[slot, rows, :], abuf.at[slot, rows, :], a_send.at[i], a_recv.at[i], (dp, ch(xr, ylo)))

    def emb_step():
        for i in range(4):
            ef[i] = ep[i].astype(F32)
        for t in range(2):
            for i in range(4):
                em[t, 20 * i:20 * i + 20, :] = ef[i, 20 * t:20 * t + 20, :]
        row0 = pl.multiple_of((80 * z) % 128, 16)
        e_w[pl.ds(row0, SLOT), 0:128] = em[0].astype(BF16)
        e_w[pl.ds(row0, SLOT), 128:256] = em[1].astype(BF16)
        for k in range(1, NZ):
            emb_in(k).wait_recv()
        e_part[...] = jnp.dot(
            e_act[...].reshape(NZ, 256).astype(BF16), e_w[...],
            preferred_element_type=F32).reshape(NZ, 1, 256)
        e_sum[z] = e_part[z]
        for k in range(1, NZ):
            part_copy(k).start()

    def stats():
        def total(lo, n, centre):
            def step(k, acc):
                v = hown[pl.ds(pl.multiple_of(lo + 128 * k, 128), 128), :].astype(F32)
                if centre is not None:
                    v = v - centre
                    v = v * v
                return acc + jnp.sum(v.reshape(16, 8, 128), axis=0)
            acc = lax.fori_loop(0, n, step, jnp.zeros((8, 128), F32))
            return jnp.sum(acc, axis=0, keepdims=True)

        def fold(v):
            v = v + pltpu.roll(v, 64, 1)
            return v + pltpu.roll(v, 32, 1)

        def fold1(v):
            return fold(jnp.broadcast_to(v, (8, 128)))[0:1, :]

        m_main = total(0, 8, None) * (1.0 / 1024.0)
        m_res = fold1(total(1024, 2, None)) * (1.0 / 1024.0)
        v_main = total(0, 8, m_main) * (1.0 / 1024.0)
        v_res = fold1(total(1024, 2, m_res)) * (1.0 / 1024.0)
        return m_main, m_res, v_main, v_res, fold1

    m_main, m_res, v_main, v_res, fold1 = stats()

    def affine():
        for k in range(1, NZ):
            part_in(k).wait_recv()
        prod = jnp.sum(e_sum[...], axis=0)
        lane = lane_iota(1)
        prm = jnp.concatenate([b_emb_ref[...], gain_ref[...], bias_ref[...]], axis=0)
        prm_res = jnp.concatenate([prm[:, 128:160]] * 4, axis=1)
        s_main = prod[0:1, 0:128] + prm[0:1, 0:128]
        s_res = fold1(jnp.where(lane < 32, prod[0:1, 128:256], 0.0)) + prm_res[0:1]
        u_main = m_main + s_main
        u_res = m_res + s_res

        def group(main, res):
            out_main = jnp.zeros((1, 128), F32)
            for g in range(3):
                inside = (lane >= 40 * g) & (lane < 40 * g + 40)
                t = jnp.sum(jnp.where(inside, main, 0.0), axis=1, keepdims=True) * (1.0 / 40.0)
                out_main = jnp.where(inside, t, out_main)
            t = jnp.sum(jnp.where(lane >= 120, main, 0.0) + jnp.where(lane < 32, res, 0.0),
                        axis=1, keepdims=True) * (1.0 / 40.0)
            return jnp.where(lane >= 120, t, out_main), jnp.broadcast_to(t, (1, 128))

        mean_main, mean_res = group(u_main, u_res)
        d_main = u_main - mean_main
        d_res = u_res - mean_res
        var_main, var_res = group(v_main + d_main * d_main, v_res + d_res * d_res)
        a_main = prm[1:2, 0:128] * lax.rsqrt(var_main + 1e-5)
        a_res = prm_res[1:2] * lax.rsqrt(var_res + 1e-5)
        b_main = prm[2:3, 0:128] + (s_main - mean_main) * a_main
        b_res = prm_res[2:3] + (s_res - mean_res) * a_res
        abv[me] = jnp.concatenate(
            [a_main, b_main, a_res, b_res, jnp.zeros((4, 128), F32)], axis=0)

    def ab_copy(k):
        return rcopy(abv.at[me], abv.at[me], b_send.at[k - 1], b_recv.at[k - 1], (dp, (chan + k) % 8))

    def ab_in(k):
        slot = (chan - k + 8) % 8
        return rcopy(abv.at[slot], abv.at[slot], b_send.at[k - 1], b_recv.at[k - 1], (dp, (chan + k) % 8))

    late = lax.div(z + 1, 2) + 3

    def place_of(block):
        return lax.rem(block - late + 16, 8)

    def normalise(src, slot):
        ab = abv[slot]

        def silu(v, a, b):
            v = v.astype(F32) * a + b
            half = 0.5 * v
            return half + half * jnp.tanh(half)

        lanes = pl.ds(pl.multiple_of(place_of(slot) * 128, 128), 128)

        def step(k, carry):
            rows = pl.ds(pl.multiple_of(128 * k, 128), 128)
            nt[rows, lanes] = silu(src[rows, :], ab[0:1], ab[1:2]).astype(BF16)
            return carry
        lax.fori_loop(0, 8, step, 0)

        def step_res(k, carry):
            rows = pl.ds(pl.multiple_of(1024 + 128 * k, 128), 128)
            sbuf[slot, pl.ds(pl.multiple_of(128 * k, 128), 128), :] = silu(src[rows, :], ab[2:3], ab[3:4])
            return carry
        lax.fori_loop(0, 2, step_res, 0)

    def merge_tails():
        lane = lane_iota(256)
        for k in range(4):
            for half in range(2):
                acc = jnp.zeros((256, 128), F32)
                for m in range(4):
                    v = sbuf[4 * half + m]
                    shift = (32 * (m - k)) % 128
                    if shift:
                        v = pltpu.roll(v, shift, 1)
                    acc = jnp.where((lane >= 32 * m) & (lane < 32 * m + 32), v, acc)
                nt[256 * k:256 * k + 256, 1024 + 128 * half:1152 + 128 * half] = acc.astype(BF16)

    def place(slot):
        for i in range(4):
            pf[i] = pbuf[slot, i].astype(F32)
        for t in range(TILES):
            for i in range(4):
                mf[t, 20 * i:20 * i + 20, :] = pf[i, 20 * t:20 * t + 20, :]
        j = lax.div(slot, 2)
        odd = lax.rem(slot, 2)
        main = 128 * place_of(j)
        lo = pl.multiple_of(main + 80 * odd, 16)
        hi = pl.multiple_of((1 - odd) * (main + 48) + odd * (1024 + 32 * j), 16)
        for t in range(TILES):
            cols = slice(128 * t, 128 * t + 128)
            wk[pl.ds(lo, 48), cols] = mf[t, 0:48, :].astype(BF16)
            wk[pl.ds(hi, 32), cols] = mf[t, 48:80, :].astype(BF16)

    xlb, xrb, yb_, ob = ch(xl, ylo), ch(xr, ylo), ch(x, yb), ch(xo, ylo)
    lyb, ryb, oyb = ch(xl, yb), ch(xr, yb), ch(xo, yb)

    def product(n, first):
        cols = pl.ds(pl.multiple_of(256 * n, 256), 256)
        rows = slice(PAD, PAD + 1024)
        if first:
            z_ref[rows, cols] = jnp.dot(nt[:, 256:1024], wk[256:1024, cols], preferred_element_type=F32)
        else:
            z_ref[rows, cols] += (
                jnp.dot(nt[:, 0:256], wk[0:256, cols], preferred_element_type=F32)
                + jnp.dot(nt[:, 1024:1280], wk[1024:1280, cols], preferred_element_type=F32))

    for s in range(1, 9):
        if s <= 7:
            for c in range(2):
                for d in range(2):
                    ring_in(d, 0, c, s).wait_recv()
                    if s < 7:
                        ring(d, 0, c, s + 1).start()
                    if s == 6 and d == 0:
                        ring_last(0, c).start()
                    across(d, 0, c, s).start()
        if s == 1:
            for c in range(2):
                row_in(c).wait_recv()
                for d in range(2):
                    ring(d, 1, c, 1).start()
                own_out(1, c).start()
        else:
            for c in range(2):
                for d in range(2):
                    ring_in(d, 1, c, s - 1).wait_recv()
                    if s < 8:
                        ring(d, 1, c, s).start()
                    if s == 7 and d == 1:
                        ring_last(1, c).start()
                    across(d, 1, c, s - 1).start()
        if s >= 7:
            for c in range(2):
                ring_in(s - 7, s - 7, c, 8).wait_recv()
                across(s - 7, s - 7, c, 8).start()
        if s == 1:
            row_in(2).wait_recv()
            own_out(1, 2).start()
            got(xlb, 0, 0).wait_recv()
            go(act(abuf.at[xlb], xlb, 0, ch(xr, ylo), 6))
            got(xrb, 1, 3).wait_recv()
            go(act(abuf.at[xrb], xrb, 1, ch(xl, ylo), 7))
            got(yb_, 0, 4).wait_recv()
            go(act(abuf.at[yb_], yb_, 0, ch(xr, ylo), 8))
            go(act(abuf.at[yb_], yb_, 0, ch(xl, ylo), 10))
            own_in(0, 2).wait_recv()
            own_in(1, 2).wait_recv()
            emb_step()
        if s == 2:
            got(yb_, 1, 5).wait_recv()
            go(act(abuf.at[yb_], yb_, 1, ch(xr, ylo), 9))
            go(act(abuf.at[yb_], yb_, 1, ch(xl, ylo), 11))
            affine()
            for k in range(1, 8):
                ab_copy(k).start()
        if s == 3:
            got(ob, 0, 6).wait_recv()
            go(act(abuf.at[ob], ob, 0, ch(x, yb), 12))
            got(ob, 1, 7).wait_recv()
            go(act(abuf.at[ob], ob, 1, ch(x, yb), 13))
            normalise(hown, me)
        if s == 4:
            for k in range(1, 8):
                ab_in(k).wait_recv()
            got(xlb, 1, 1).wait_recv()
            normalise(abuf.at[xlb], xlb)
            got(xrb, 0, 2).wait_recv()
            normalise(abuf.at[xrb], xrb)
        if s == 5:
            normalise(abuf.at[yb_], yb_)
            normalise(abuf.at[ob], ob)
        if s == 6:
            got(lyb, 0, 8).wait_recv()
            got(lyb, 1, 9).wait_recv()
            normalise(abuf.at[lyb], lyb)
            got(ryb, 0, 10).wait_recv()
            got(ryb, 1, 11).wait_recv()
            normalise(abuf.at[ryb], ryb)
            got(oyb, 0, 12).wait_recv()
            got(oyb, 1, 13).wait_recv()
            normalise(abuf.at[oyb], oyb)
        if s == 1:
            for r in range(2):
                for c in range(2):
                    own_in(r, c).wait_recv()
            place(z)
        elif s < 8:
            for d in range(2):
                for r in range(2):
                    for c in range(2):
                        across_in(d, r, c, s - 1).wait_recv()
                place(plane(d, s - 1))
        if s == 7:
            def early(n, carry):
                product(n, True)
                return carry
            lax.fori_loop(0, 6, early, 0)
            merge_tails()

    for d in range(2):
        for r in range(2):
            for c in range(2):
                across_in(d, r, c, 7).wait_recv()
        place(plane(d, 7))
    for c in range(2):
        across_in(0, 0, c, 8).wait_recv()
        across_in(1, 1, c, 8).wait_recv()
    place(plane(0, 8))

    z_ref[0:PAD, :] = jnp.zeros((PAD, 1536), F32)
    z_ref[PAD + 1024:PAD + 1024 + PAD, :] = jnp.zeros((PAD, 1536), F32)

    def late_part(n, carry):
        product(n, False)
        return carry
    lax.fori_loop(0, 6, late_part, 0)

    loads[3].wait()
    bias_main = b_conv_ref[:, 0:128]
    bias_res = jnp.concatenate([b_conv_ref[:, 128:160]] + [jnp.zeros((1, 96), F32)], axis=1)
    row = lax.broadcasted_iota(jnp.int32, (128, 128), 0) % 32
    lane = lane_iota(128)
    for k in range(8):
        base = PAD + 128 * k

        def band(tile, off):
            return z_ref[base + off:base + off + 128, 128 * tile:128 * tile + 128]

        side = [jnp.zeros((128, 128), F32)] * 3
        for dx in range(3):
            for dy in range(3):
                side[dx] = side[dx] + band(3 + 3 * dy + dx, 32 * (dy - 1) + dx - 1)
        main = side[1] + jnp.where(row > 0, side[0], 0.0) + jnp.where(row < 31, side[2], 0.0)
        res = [sum(band(dy, 32 * (dy - 1) + off) for dy in range(3)) for off in (-1, 0, 1)]
        u = jnp.where(lane < 32, jnp.where(row > 0, res[0], 0.0),
                      jnp.where(lane < 64, res[1],
                                jnp.where((lane < 96) & (row < 31), res[2], 0.0)))
        u = u + pltpu.roll(u, 96, 1) + pltpu.roll(u, 64, 1)
        cols = slice(128 * k, 128 * k + 128)
        out_ref[0:128, cols] = (skip_ref[0:128, cols].astype(F32) + (main + bias_main).T).astype(BF16)
        tail = (u + bias_res).T
        out_ref[128:160, cols] = (skip_ref[128:160, cols].astype(F32) + tail[0:32, :]).astype(BF16)

    for c in range(3):
        row_out(c).wait_send()
        own_out(0, c).wait_send()
        own_out(1, c).wait_send()
    for copy in sent:
        copy.wait_send()
    for k in range(1, 8):
        ab_copy(k).wait_send()
    for k in range(1, NZ):
        emb_copy(k).wait_send()
        part_copy(k).wait_send()
    for d in range(2):
        for c in range(2):
            for r in range(2):
                for s in range(1, 8):
                    ring(d, r, c, s).wait_send()
                    across(d, r, c, s).wait_send()
            ring_last(d, c).wait_send()
            across(d, d, c, 8).wait_send()


def body(h_in, skip, emb, w_emb, b_emb, gn_gain, gn_bias, w_conv, b_conv):
    rows = [v[None] for v in (b_emb, gn_gain, gn_bias, b_conv)]
    vmem = pl.BlockSpec(memory_space=pltpu.VMEM)
    hbm = pl.BlockSpec(memory_space=pltpu.MemorySpace.HBM)
    dma = pltpu.SemaphoreType.DMA
    out = pl.pallas_call(
        kernel,
        out_shape=jax.ShapeDtypeStruct((160, 1024), BF16),
        in_specs=[hbm, hbm, vmem, hbm, vmem, vmem, vmem, vmem, hbm],
        out_specs=vmem,
        scratch_shapes=[
            pltpu.VMEM((160, 1024), BF16),
            pltpu.VMEM((160, 1024), BF16),
            pltpu.VMEM((20, 160), BF16),
            pltpu.VMEM((9, 20, 160), BF16),
            pltpu.VMEM((ROWS, 128), BF16),
            pltpu.VMEM((NZ, 4, PIECE, 128), BF16),
            pltpu.VMEM((4, PIECE, 128), F32),
            pltpu.VMEM((TILES, SLOT, 128), F32),
            pltpu.VMEM((4, EP, 128), BF16),
            pltpu.VMEM((4, EP, 128), F32),
            pltpu.VMEM((2, SLOT, 128), F32),
            pltpu.VMEM((1280, 1536), BF16),
            pltpu.VMEM((8, ROWS, 128), BF16),
            pltpu.VMEM((1024, 1280), BF16),
            pltpu.VMEM((8, 256, 128), F32),
            pltpu.VMEM((8, 8, 128), F32),
            pltpu.VMEM((1024 + 2 * PAD, 1536), F32),
            pltpu.VMEM((1, 1408), F32),
            pltpu.VMEM((NZ, 1, 256), F32),
            pltpu.VMEM((256, 256), BF16),
            pltpu.VMEM((NZ, 1, 256), F32),
            pltpu.VMEM((NZ, 1, 256), F32),
            dma((4,)),
            dma((3,)), dma((3,)), dma((6,)), dma((6,)),
            dma((64,)), dma((64,)), dma((64,)), dma((64,)),
            dma((14,)), dma((14,)),
            dma((7,)), dma((7,)),
            dma((15,)), dma((15,)), dma((15,)), dma((15,)),
        ],
        compiler_params=pltpu.CompilerParams(
            collective_id=0, has_side_effects=True, vmem_limit_bytes=56 << 20),
        name="resblock",
    )(h_in, skip, emb, w_emb, *rows, w_conv)
    return out[None]


def solution(mesh):
    return jax.shard_map(
        body,
        mesh=mesh,
        in_specs=(
            P("dp", "chan", None),
            P("dp", "chan", None),
            P("dp", None),
            P("dp", "chan"),
            P("chan"),
            P("chan"),
            P("chan"),
            P(None, "dp", "chan"),
            P("chan"),
        ),
        out_specs=P("dp", "chan", None),
        check_vma=False,
    )
```
